128 devices in a mesh: dev: 128 (over x, z, y, core).
Axes of the slice: x: 4, y: 4, z: 4, core: 2. Of those that a mesh axis runs over, the one named last changes fastest.
Arguments:
- log_depth: float32 [1024, 12544], P('dev'), may hold values from -1.5 to 1.5
- depth_m: float32 [1024, 12544], P('dev'), may hold values from -0.006 to 0.006
- depth_v: float32 [1024, 12544], P('dev'), may hold values from 1e-07 to 1e-05
- image_params: float32 [7, 1024], P(None, 'dev'), may hold values from -1.5 to 1.5
- image_m: float32 [7, 1024], P(None, 'dev'), may hold values from -6 to 6
- image_v: float32 [7, 1024], P(None, 'dev'), may hold values from 0.1 to 10
- pair_points: bfloat16 [3072, 2, 3, 12544], P('dev'), may hold values from -6 to 6
- pair_conf: bfloat16 [3072, 2, 12544], P('dev'), may hold values from 1 to 5
- pair_params: float32 [7, 3072], P(None, 'dev'), may hold values from -1.5 to 1.5
- pair_m: float32 [7, 3072], P(None, 'dev'), may hold values from -6 to 6
- pair_v: float32 [7, 3072], P(None, 'dev'), may hold values from 0.1 to 10
- fetch: int32 [128, 9], P('dev'), may hold values from 0 to 7
- pair_sides: int32 [3072, 2], P('dev'), may hold values from 0 to 8, as said below
- pair_count: int32 [128], P('dev'), may hold values from 6 to 24, as said below
Outputs:
- new_depth: float32 [1024, 12544], P('dev')
- new_image_params: float32 [7, 1024], P(None, 'dev')
- new_pair_params: float32 [7, 3072], P(None, 'dev')
The draws below stay inside these ranges and needn't reach their ends.
Inputs may be any that keep to these rules, and one draw needn't show every extreme that they name: `pair_sides`: the two positions of a slot differ. The first slot of every holder has second position 8. `pair_count`: each holder has at least a quarter of its slots live, and some holder has all 24 live.
All inputs are finite; a program needn't handle non-finite values.
Results may differ from the reference program's by a relative error of at most 0.0003.
Values may be sent and summed in bfloat16 or wider, within the bound.
No kernel may reach another device: no remote copies, remote signals or barrier semaphores. Data moves between devices by JAX's collectives and lax.ppermute only.
A program may use at most 128 MiB of HBM per device.

```python
import math
import jax
import jax.numpy as jnp
from jax import lax

IMG_SIDE = 112
PIX = 12544
IMG_DEV = 8
SLOTS = 24
REACH = 4
ITERS = 2
HOLDERS = 128
IMAGES = 1024
PAIRS = 3072


def draw_pair_sides(key, part):
    width_k = 2 * REACH + 1
    first_key = jax.random.fold_in(key, 11)
    second_key = jax.random.fold_in(key, 12)
    lead_key = jax.random.fold_in(key, 13)
    first = jax.random.randint(first_key, (PAIRS,), 0, width_k)
    stride = jax.random.randint(second_key, (PAIRS,), 1, width_k)
    second = (first + stride) % width_k
    lead_first = jax.random.randint(lead_key, (PAIRS,), 0, width_k - 1)
    is_lead = jnp.arange(PAIRS) % SLOTS == 0
    first = jnp.where(is_lead, lead_first, first)
    second = jnp.where(is_lead, width_k - 1, second)
    return jnp.stack([first, second], axis=1).astype(jnp.int32)


def draw_pair_count(key, part):
    count_key = jax.random.fold_in(key, 21)
    full_key = jax.random.fold_in(key, 22)
    counts = jax.random.randint(count_key, (HOLDERS,), max(SLOTS // 4, 1), SLOTS + 1)
    full = jax.random.randint(full_key, (), 0, HOLDERS)
    return jnp.where(jnp.arange(HOLDERS) == full, SLOTS, counts).astype(jnp.int32)


def touch_ends(values, own_key, low, largest):
    shape = values.shape
    spot = [jax.random.randint(jax.random.fold_in(own_key, axis), (), 0, shape[axis]) for axis in range(len(shape))]
    values = values.at[tuple(spot)].set(low)
    longest = shape.index(max(shape))
    spot[longest] = (spot[longest] + 1) % shape[longest]
    return values.at[tuple(spot)].set(largest)


def levels(rng, extent, split, smallest, largest):
    def one(dim, blocks):
        draws = jax.random.uniform(jax.random.fold_in(jax.random.fold_in(rng, 6), dim), (blocks,), jnp.float32, smallest / len(split), largest / len(split))
        return jnp.repeat(jnp.exp(draws), extent[dim] // blocks).reshape((-1,) + (1,) * (len(extent) - dim - 1))

    factor_of = one(*split[0])
    for cut in split[1:]:
        factor_of = factor_of * one(*cut)
    return factor_of


def centred(own_key, dims, scale, most, shards=(), held_as=jnp.bfloat16):
    values = jax.random.normal(own_key, dims, jnp.float32) * scale
    if len(shards) > 0:
        values = levels(own_key, dims, shards, -0.22, 0.18) * values
    return jnp.clip(values, min=-most, max=most).astype(held_as)


def setup_inputs(seed: int = 0) -> dict:
    arg_keys = jax.random.split(jax.random.key(seed), 15)
    log_depth = centred(arg_keys[0], (IMAGES, PIX), 0.3, 1.5, ((0, 128),), jnp.float32)
    depth_m = centred(arg_keys[1], (IMAGES, PIX), 0.001, 0.006, ((0, 128),), jnp.float32)
    depth_v = jnp.clip(jnp.exp(math.log(9.999999747378752e-06) - 4.6051701 * jax.random.uniform(arg_keys[2], (IMAGES, PIX), jnp.float32) ** levels(arg_keys[2], (IMAGES, PIX), ((0, 128),), -0.2, 0.2)), 1.0000000116860974e-07, 9.999999747378752e-06)
    image_params = centred(arg_keys[3], (7, IMAGES), 0.3, 1.5, ((1, 128),), jnp.float32)
    image_m = centred(arg_keys[4], (7, IMAGES), 1.0, 6.0, ((1, 128),), jnp.float32)
    image_v = jnp.clip(jnp.exp(math.log(10.0) - 4.6051702 * jax.random.uniform(arg_keys[5], (7, IMAGES), jnp.float32) ** levels(arg_keys[5], (7, IMAGES), ((1, 128),), -0.2, 0.2)), 0.1, 10.0)
    pair_points = centred(arg_keys[6], (PAIRS, 2, 3, PIX), 1.0, 6.0, ((0, 128),))
    pair_conf = jnp.clip(jnp.exp(math.log(5.0) - 1.609438 * jax.random.uniform(arg_keys[7], (PAIRS, 2, PIX), jnp.float32) ** levels(arg_keys[7], (PAIRS, 2, PIX), ((0, 128),), -0.2, 0.2)), 1.0, 5.0).astype(jnp.bfloat16)
    pair_params = centred(arg_keys[8], (7, PAIRS), 0.3, 1.5, ((1, 128),), jnp.float32)
    pair_m = centred(arg_keys[9], (7, PAIRS), 1.0, 6.0, ((1, 128),), jnp.float32)
    pair_v = jnp.clip(jnp.exp(math.log(10.0) - 4.6051702 * jax.random.uniform(arg_keys[10], (7, PAIRS), jnp.float32) ** levels(arg_keys[10], (7, PAIRS), ((1, 128),), -0.2, 0.2)), 0.1, 10.0)
    fetch = touch_ends(jax.random.randint(arg_keys[11], (HOLDERS, 2 * REACH + 1), 0, IMG_DEV), jax.random.fold_in(arg_keys[11], 1), 0, IMG_DEV - 1).astype(jnp.int32)
    pair_sides = draw_pair_sides(jax.random.fold_in(arg_keys[14], 71), 0)
    pair_count = draw_pair_count(jax.random.fold_in(arg_keys[14], 71), 0)
    return dict(log_depth=log_depth, depth_m=depth_m, depth_v=depth_v, image_params=image_params, image_m=image_m, image_v=image_v, pair_points=pair_points, pair_conf=pair_conf, pair_params=pair_params, pair_m=pair_m, pair_v=pair_v, fetch=fetch, pair_sides=pair_sides, pair_count=pair_count)


focal_base = 100.0
learn_rate = 0.05
beta_one = 0.9
beta_two = 0.999
adam_epsilon = 1e-08
adam_start = 20

def rotation(vector):
    xval, yval, zval = (vector[0], vector[1], vector[2])
    scale = 1.0 / (1.0 + xval * xval + yval * yval + zval * zval)
    return [[(1.0 + xval * xval - yval * yval - zval * zval) * scale, 2.0 * (xval * yval - zval) * scale, 2.0 * (xval * zval + yval) * scale], [2.0 * (xval * yval + zval) * scale, (1.0 - xval * xval + yval * yval - zval * zval) * scale, 2.0 * (yval * zval - xval) * scale], [2.0 * (xval * zval - yval) * scale, 2.0 * (yval * zval + xval) * scale, (1.0 - xval * xval - yval * yval + zval * zval) * scale]]

def residual_loss(depth_terms, image_terms, pair_terms, points, confidence, weight):
    total = depth_terms.shape[1]
    position = jnp.arange(total, dtype=jnp.int32)
    centre = (IMG_SIDE - 1) / 2.0
    column_pos = (position % IMG_SIDE).astype(jnp.float32) - centre
    row_pos = (position // IMG_SIDE).astype(jnp.float32) - centre
    focal = focal_base * jnp.exp(image_terms[6])[:, None]
    depth = jnp.exp(depth_terms)
    camera = (depth * column_pos[None, :] / focal, depth * row_pos[None, :] / focal, depth)
    spin = rotation(image_terms[0:3])
    turn = rotation(pair_terms[0:3])
    scale = jnp.exp(pair_terms[6])[:, None]
    squared = jnp.zeros_like(depth)
    for axis_id in range(3):
        world = spin[axis_id][0][:, None] * camera[0] + spin[axis_id][1][:, None] * camera[1] + spin[axis_id][2][:, None] * camera[2] + image_terms[3 + axis_id][:, None]
        target = scale * (turn[axis_id][0][:, None] * points[:, 0] + turn[axis_id][1][:, None] * points[:, 1] + turn[axis_id][2][:, None] * points[:, 2] + pair_terms[3 + axis_id][:, None])
        squared = squared + (world - target) * (world - target)
    per_term = lax.optimization_barrier(jnp.mean(confidence * squared, axis=1))
    return jnp.sum(weight * per_term)

def adam_step(param, grad, moment, second, count):
    moment = beta_one * moment + (1.0 - beta_one) * grad
    second = beta_two * second + (1.0 - beta_two) * grad * grad
    fix_one = 1.0 - beta_one ** count
    fix_two = 1.0 - beta_two ** count
    param = param - learn_rate * (moment / fix_one) / (jnp.sqrt(second / fix_two) + adam_epsilon)
    return (param, moment, second)

def reference(log_depth, depth_m, depth_v, image_params, image_m, image_v, pair_points, pair_conf, pair_params, pair_m, pair_v, fetch, pair_sides, pair_count):
    width_k = 2 * REACH + 1
    points_all = pair_points.reshape(HOLDERS, SLOTS, 2, 3, PIX)
    conf_all = pair_conf.reshape(HOLDERS, SLOTS, 2, PIX)
    sides_all = pair_sides.reshape(HOLDERS, SLOTS, 2)
    holder_ids = jnp.arange(HOLDERS, dtype=jnp.int32)
    window_pos = jnp.arange(width_k, dtype=jnp.int32)
    offsets = jnp.where(window_pos < 2 * REACH, window_pos - REACH, HOLDERS // 2).astype(jnp.int32)
    for step_id in range(ITERS):
        depth_used = lax.optimization_barrier(log_depth.astype(jnp.bfloat16)).astype(jnp.float32)
        params_used = lax.optimization_barrier(image_params.astype(jnp.bfloat16)).astype(jnp.float32)
        pair_blocks = pair_params.reshape(7, HOLDERS, SLOTS).transpose(1, 0, 2)

        def holder_step(carry, inputs):
            grad_depth, grad_params = carry
            holder, points, confidence, pair_block, fetch_row, sides, count = inputs
            owners = ((holder + offsets) % HOLDERS).astype(jnp.int32)
            image_ids = (owners * IMG_DEV + fetch_row).astype(jnp.int32)
            flat_ids = image_ids[sides.reshape(-1)]
            depth_terms = depth_used[flat_ids]
            image_terms = params_used[:, flat_ids]
            live = (jnp.arange(SLOTS, dtype=jnp.int32) < count).astype(jnp.float32)
            weight = jnp.repeat(live, 2)
            points_flat = points.reshape(2 * SLOTS, 3, PIX).astype(jnp.float32)
            conf_flat = confidence.reshape(2 * SLOTS, PIX).astype(jnp.float32)

            def loss_of(depth_in, params_in, pair_in):
                return residual_loss(depth_in, params_in, jnp.repeat(pair_in, 2, axis=1), points_flat, conf_flat, weight)
            value, pullback = jax.vjp(loss_of, depth_terms, image_terms, pair_block)
            grad_terms, grad_image, grad_pair = pullback(jnp.float32(1.0))
            grad_depth = grad_depth.at[flat_ids].add(grad_terms)
            grad_params = grad_params.at[:, flat_ids].add(grad_image)
            return ((grad_depth, grad_params), grad_pair)
        start = (jnp.zeros((IMAGES, PIX), jnp.float32), jnp.zeros((7, IMAGES), jnp.float32))
        (grad_depth, grad_params), grad_pairs = lax.scan(holder_step, start, (holder_ids, points_all, conf_all, pair_blocks, fetch, sides_all, pair_count))
        grad_pair = grad_pairs.transpose(1, 0, 2).reshape(7, PAIRS)
        count = adam_start + step_id + 1
        log_depth, depth_m, depth_v = adam_step(log_depth, grad_depth, depth_m, depth_v, count)
        image_params, image_m, image_v = adam_step(image_params, grad_params, image_m, image_v, count)
        pair_params, pair_m, pair_v = adam_step(pair_params, grad_pair, pair_m, pair_v, count)
    return (log_depth, image_params, pair_params)
```

```python
import jax
import jax.numpy as jnp
from jax import lax
from jax.experimental import pallas as pl
from jax.experimental.pallas import tpu as pltpu
from jax.sharding import PartitionSpec as P

IMG_SIDE = 112
PIX = 12544
REACH = 4
ITERS = 2
WIDTH = 2 * REACH + 1
CHUNKS = PIX // 128
PROW = 112
RS = 104
NB = 1792
STEPS = PIX // NB
SUB = NB // 128
TERMS = 48
CROWS = 7 * TERMS
FCOLS = 176

focal_base = 100.0
learn_rate = 0.05
beta_one = 0.9
beta_two = 0.999
adam_epsilon = 1e-08
adam_start = 20


F32 = jnp.float32
BF16 = jnp.bfloat16
HIGH = lax.Precision.HIGHEST


def adam(param, grad, moment, second, count):
    moment = beta_one * moment + (1.0 - beta_one) * grad
    second = beta_two * second + (1.0 - beta_two) * grad * grad
    fix_one = 1.0 - beta_one**count
    fix_two = 1.0 - beta_two**count
    step = (learn_rate / fix_one) * moment / (jnp.sqrt(second * (1.0 / fix_two)) + adam_epsilon)
    return param - step, moment, second


def rotation(vec):
    x, y, z = vec
    s = 1.0 / (1.0 + x * x + y * y + z * z)
    return [
        [(1.0 + x * x - y * y - z * z) * s, 2.0 * (x * y - z) * s, 2.0 * (x * z + y) * s],
        [2.0 * (x * y + z) * s, (1.0 - x * x + y * y - z * z) * s, 2.0 * (y * z - x) * s],
        [2.0 * (x * z - y) * s, 2.0 * (y * z + x) * s, (1.0 - x * x - y * y + z * z) * s],
    ], s


def rotation_grad(vec, rot, s, g):
    x, y, z = vec
    inner = sum(g[i][j] * rot[i][j] for i in range(3) for j in range(3))
    s2 = 2.0 * s
    gx = x * (g[0][0] - g[1][1] - g[2][2]) + y * (g[0][1] + g[1][0]) + z * (g[0][2] + g[2][0]) + (g[2][1] - g[1][2])
    gy = y * (g[1][1] - g[0][0] - g[2][2]) + x * (g[0][1] + g[1][0]) + z * (g[1][2] + g[2][1]) + (g[0][2] - g[2][0])
    gz = z * (g[2][2] - g[0][0] - g[1][1]) + x * (g[0][2] + g[2][0]) + y * (g[1][2] + g[2][1]) + (g[1][0] - g[0][1])
    return [s2 * (gx - x * inner), s2 * (gy - y * inner), s2 * (gz - z * inner)]


def split(value):
    high = value.astype(BF16).astype(F32)
    return high, value - high


def nt(lhs, rhs, precision=None):
    return lax.dot_general(lhs, rhs, (((1,), (1,)), ((), ())), precision=precision, preferred_element_type=F32)


def nn(lhs, rhs, precision=None):
    return lax.dot_general(lhs, rhs, (((1,), (0,)), ((), ())), precision=precision, preferred_element_type=F32)


def iota(shape, dim):
    return lax.broadcasted_iota(jnp.int32, shape, dim)


def prepare_kernel(points_ref, conf_ref, out_ref, sums_ref, acc_ref):
    step = pl.program_id(0)

    @pl.when(step == 0)
    def _():
        acc_ref[...] = jnp.zeros_like(acc_ref)

    conf = conf_ref[...]
    out_ref[0:TERMS, :] = conf
    conf = conf.astype(F32)
    pts = [points_ref[d].astype(F32) for d in range(3)]
    weighted = [conf * pts[d] for d in range(3)]
    for d in range(3):
        high, low = split(weighted[d])
        out_ref[(1 + d) * TERMS : (2 + d) * TERMS, :] = high.astype(BF16)
        out_ref[(4 + d) * TERMS : (5 + d) * TERMS, :] = low.astype(BF16)
    j = 0
    for a in range(3):
        for b in range(a, 3):
            prod = weighted[a] * pts[b]
            total = prod[:, 0:128]
            for c in range(1, SUB):
                total = total + prod[:, c * 128 : (c + 1) * 128]
            acc_ref[j] += total
            j += 1

    @pl.when(step == STEPS - 1)
    def _():
        lane = iota((TERMS, 128), 1)
        res = jnp.zeros((TERMS, 128), F32)
        for i in range(6):
            res = jnp.where(lane == i, jnp.sum(acc_ref[i], axis=1, keepdims=True), res)
        sums_ref[...] = res


def prepare(points, conf):
    return pl.pallas_call(
        prepare_kernel,
        grid=(STEPS,),
        in_specs=[
            pl.BlockSpec((3, TERMS, NB), lambda i: (0, 0, i)),
            pl.BlockSpec((TERMS, NB), lambda i: (0, i)),
        ],
        out_specs=[
            pl.BlockSpec((CROWS, NB), lambda i: (0, i)),
            pl.BlockSpec((TERMS, 128), lambda i: (0, 0)),
        ],
        out_shape=[
            jax.ShapeDtypeStruct((CROWS, PIX), BF16),
            jax.ShapeDtypeStruct((TERMS, 128), F32),
        ],
        scratch_shapes=[pltpu.VMEM((6, TERMS, 128), F32)],
        compiler_params=pltpu.CompilerParams(vmem_limit_bytes=24 << 20),
        cost_estimate=pl.CostEstimate(flops=20_000_000, bytes_accessed=14_000_000, transcendentals=0),
        name="prepare",
    )(points, conf)


def pick_payloads(served, rows_ref, param_rows, out_refs):
    pad = jnp.zeros((PROW - CHUNKS, 128), F32)
    for k in range(WIDTH):
        image = served[k]
        pixels = rows_ref[pl.ds(image, CHUNKS, stride=8), :]
        row = param_rows[pl.ds(image, 1), :]
        tail = jnp.where(iota((PROW - CHUNKS, 128), 0) == 0, row, pad)
        out_refs[k][...] = jnp.concatenate([pixels, tail], axis=0).astype(BF16)


def served_images(served_refs):
    return [served_refs[k][0, k] for k in range(WIDTH)]


def first_kernel(*refs):
    served = served_images(refs[:WIDTH])
    depth_ref, param_ref = refs[WIDTH : WIDTH + 2]
    outs = refs[WIDTH + 2 : 2 * WIDTH + 2]
    rows_ref = refs[2 * WIDTH + 2]
    for c in range(CHUNKS):
        rows_ref[8 * c : 8 * c + 8, :] = depth_ref[:, 128 * c : 128 * c + 128]
    pick_payloads(served, rows_ref, param_ref, outs)


def first(served, depth, params):
    return pl.pallas_call(
        first_kernel,
        in_specs=[pl.BlockSpec(memory_space=pltpu.SMEM)] * WIDTH + [pl.BlockSpec(memory_space=pltpu.VMEM)] * 2,
        out_specs=[pl.BlockSpec(memory_space=pltpu.VMEM)] * WIDTH,
        out_shape=[jax.ShapeDtypeStruct((PROW, 128), BF16)] * WIDTH,
        scratch_shapes=[pltpu.VMEM((8 * CHUNKS, 128), F32)],
        compiler_params=pltpu.CompilerParams(vmem_limit_bytes=16 << 20),
        cost_estimate=pl.CostEstimate(flops=1_000_000, bytes_accessed=700_000, transcendentals=0),
        name="first",
    )(*served, depth, params)


def update_kernel(count, last, *refs):
    served = served_images(refs[:WIDTH])
    back = refs[WIDTH : 2 * WIDTH]
    depth_ref, m_ref, v_ref, ip_ref, im_ref, iv_ref = refs[2 * WIDTH : 2 * WIDTH + 6]
    rest = refs[2 * WIDTH + 6 :]
    n_out = 2 if last else 6 + WIDTH
    outs = rest[:n_out]
    acc_ref, pacc_ref = rest[n_out : n_out + 2]
    acc_ref[...] = jnp.zeros_like(acc_ref)
    pacc_ref[...] = jnp.zeros_like(pacc_ref)
    for k in range(WIDTH):
        image = served[k]
        value = back[k][...].astype(F32)
        where = pl.ds(image, CHUNKS, stride=8)
        acc_ref[where, :] = acc_ref[where, :] + value[0:CHUNKS]
        pacc_ref[pl.ds(image, 1), :] = pacc_ref[pl.ds(image, 1), :] + value[CHUNKS : CHUNKS + 1]
    for c in range(CHUNKS):
        cols = slice(128 * c, 128 * c + 128)
        rows = slice(8 * c, 8 * c + 8)
        depth, m, v = adam(depth_ref[:, cols], acc_ref[rows, :], m_ref[:, cols], v_ref[:, cols], count)
        outs[0][:, cols] = depth
        if not last:
            outs[2][:, cols] = m
            outs[3][:, cols] = v
            acc_ref[rows, :] = depth
    param, pm, pv = adam(ip_ref[...], pacc_ref[...], im_ref[...], iv_ref[...], count)
    outs[1][...] = param
    if not last:
        outs[4][...] = pm
        outs[5][...] = pv
        pick_payloads(served, acc_ref, outs[1], outs[6:])


def update(count, last, served, back, depth, m, v, ip, im, iv):
    big = jax.ShapeDtypeStruct((8, PIX), F32)
    small = jax.ShapeDtypeStruct((8, 128), F32)
    shapes = [big, small] if last else [big, small, big, big, small, small] + [jax.ShapeDtypeStruct((PROW, 128), BF16)] * WIDTH
    vm = pl.BlockSpec(memory_space=pltpu.VMEM)
    return pl.pallas_call(
        lambda *refs: update_kernel(count, last, *refs),
        in_specs=[pl.BlockSpec(memory_space=pltpu.SMEM)] * WIDTH + [vm] * (WIDTH + 6),
        out_specs=[vm] * len(shapes),
        out_shape=shapes,
        scratch_shapes=[pltpu.VMEM((8 * CHUNKS, 128), F32), pltpu.VMEM((8, 128), F32)],
        compiler_params=pltpu.CompilerParams(vmem_limit_bytes=16 << 20),
        cost_estimate=pl.CostEstimate(flops=3_000_000, bytes_accessed=2_500_000, transcendentals=0),
        name="update",
    )(*served, *back, depth, m, v, ip, im, iv)


def grads_kernel(count_step, *refs):
    bufs = refs[:WIDTH]
    crows_ref, sums_ref, sides_col_ref, sides_row_ref, live_ref, pp_ref, pm_ref, pv_ref = refs[WIDTH : WIDTH + 8]
    outs = refs[WIDTH + 8 : 2 * WIDTH + 8]
    npp_ref, npm_ref, npv_ref = refs[2 * WIDTH + 8 : 2 * WIDTH + 11]
    depth_ref, grad_ref, coef_ref, mom_ref, ip_ref, term_ref = refs[2 * WIDTH + 11 :]
    step = pl.program_id(0)
    kappa = 2.0 / PIX

    def hot_of():
        return (iota((16, TERMS), 0) == sides_row_ref[...]).astype(F32)

    def term_rows():
        return [term_ref[i : i + 1, :] for i in range(16)]

    @pl.when(step == 0)
    def _():
        ip_ref[...] = jnp.zeros_like(ip_ref)
        for k in range(WIDTH):
            value = bufs[k][...].astype(F32)
            depth_ref[k * RS : k * RS + CHUNKS, :] = value[0:CHUNKS]
            ip_ref[k : k + 1, :] = value[CHUNKS : CHUNKS + 1]
        mom_ref[...] = jnp.zeros_like(mom_ref)
        hot = hot_of()
        images = lax.dot_general(ip_ref[...], hot, (((0,), (0,)), ((), ())), precision=HIGH, preferred_element_type=F32)
        spread = (iota((24, TERMS), 0) == iota((24, TERMS), 1) // 2).astype(F32)
        pairs = nn(pp_ref[...], spread, HIGH)
        term_ref[0:8, :] = images[0:8, :]
        term_ref[8:15, :] = pairs
        t = term_rows()
        rot, _ = rotation(t[0:3])
        turn, _ = rotation(t[8:11])
        sigma = jnp.exp(t[14])
        live = (iota((1, TERMS), 1) // 2 < live_ref[0]).astype(F32) * kappa
        tau = [t[3 + a] - sigma * t[11 + a] for a in range(3)]
        zero = jnp.zeros((16, TERMS), F32)
        blocks = []
        for j in range(3):
            a_j = (rot[0][j] * tau[0] + rot[1][j] * tau[1] + rot[2][j] * tau[2]) * live
            b_j = [
                -(rot[0][j] * turn[0][d] + rot[1][j] * turn[1][d] + rot[2][j] * turn[2][d]) * sigma * live
                for d in range(3)
            ]
            blocks.append([hot * a_j] + [hot * b for b in b_j])
        blocks.append([hot * live, zero, zero, zero])
        for j in range(4):
            for n in range(4):
                high, low = split(blocks[j][n])
                for where in ([n] if n == 0 else [n, n + 3]):
                    coef_ref[16 * j : 16 * j + 16, where * TERMS : (where + 1) * TERMS] = high
                    coef_ref[64 + 16 * j : 80 + 16 * j, where * TERMS : (where + 1) * TERMS] = low

    pos = (iota((8, NB), 1) + step * NB).astype(F32)
    row = jnp.floor((pos + 0.5) * (1.0 / IMG_SIDE))
    x = pos - row * IMG_SIDE - (IMG_SIDE - 1) / 2.0
    y = row - (IMG_SIDE - 1) / 2.0
    near = jnp.concatenate([depth_ref[pl.ds(step * SUB + c, 8, stride=RS), :] for c in range(SUB)], axis=1)
    far = jnp.concatenate([depth_ref[pl.ds(8 * RS + step * SUB + c, 1), :] for c in range(SUB)], axis=1)
    near = jnp.exp(near)
    far = jnp.exp(far)
    near2 = near * near
    fields = [near, near * x, near * y, near2, near2 * x, near2 * y]
    fields += [fields[4] * x, fields[4] * y, fields[5] * y]
    sub = iota((8, NB), 0)
    farb = jnp.broadcast_to(far, (8, NB))
    base = jnp.where(sub < 3, farb, farb * farb)
    first_w = jnp.where((sub == 1) | (sub == 4), x, jnp.where((sub == 2) | (sub == 5), y, 1.0))
    first_w = jnp.where(sub >= 6, x, first_w)
    second_w = jnp.where(sub == 6, x, jnp.where(sub == 7, y, 1.0))
    fields.append(base * first_w * second_w)
    fields.append(jnp.where(sub == 0, farb * farb * y * y, jnp.where(sub == 1, 1.0, 0.0)))
    tiles = []
    for value in fields:
        high, low = split(value)
        tiles.append(jnp.concatenate([high, low], axis=0).astype(BF16))
    stack = jnp.concatenate(tiles, axis=0)
    crows = crows_ref[...]
    mom_ref[...] += nt(crows, stack)

    out = nn(coef_ref[...].astype(BF16), crows)
    out = out[0:64] + out[64:128]
    inv_f = 1.0 / (focal_base * jnp.exp(ip_ref[:, 6:7]))
    near_f = inv_f[0:8]
    far_f = inv_f[8:9]
    rr = x * x + y * y
    near_g = near * (near * (rr * (near_f * near_f) + 1.0) * out[48:56] + (x * out[0:8] + y * out[16:24]) * near_f + out[32:40])
    far_g = far * (
        far * (rr[0:1] * (far_f * far_f) + 1.0) * out[56:57] + (x[0:1] * out[8:9] + y[0:1] * out[24:25]) * far_f + out[40:41]
    )
    for c in range(SUB):
        grad_ref[pl.ds(step * SUB + c, 8, stride=RS), :] = near_g[:, 128 * c : 128 * c + 128]
        grad_ref[pl.ds(8 * RS + step * SUB + c, 1), :] = far_g[:, 128 * c : 128 * c + 128]

    @pl.when(step == STEPS - 1)
    def _():
        col = iota((TERMS, FCOLS), 1)
        image_of = jnp.where(col < 144, col % 8, 8)
        mask = ((image_of == sides_col_ref[...]) | (col == 161)).astype(F32)
        fcol = iota((16, FCOLS), 1)
        inside = jnp.where(
            fcol < 144,
            fcol // 16,
            jnp.where(fcol < 160, fcol % 8, jnp.where(fcol % 8 == 0, 8, jnp.where(fcol == 161, 9, 20))),
        )
        pickf = (inside == iota((16, FCOLS), 0)).astype(F32)
        groups = [nt(pickf, mom_ref[0:TERMS, :] * mask, HIGH)]
        for d in range(3):
            both = mom_ref[(1 + d) * TERMS : (2 + d) * TERMS, :] + mom_ref[(4 + d) * TERMS : (5 + d) * TERMS, :]
            groups.append(nt(pickf, both * mask, HIGH))
        eye = (iota((8, 128), 0) == iota((8, 128), 1)).astype(F32)
        pp = nt(eye, sums_ref[...], HIGH)

        def at(group, field):
            return groups[group][field : field + 1, :]

        t = term_rows()
        rot, rot_s = rotation(t[0:3])
        turn, turn_s = rotation(t[8:11])
        sigma = jnp.exp(t[14])
        inv = 1.0 / (focal_base * jnp.exp(t[6]))
        inv2 = inv * inv
        live = (iota((1, TERMS), 1) // 2 < live_ref[0]).astype(F32) * kappa
        tau = [t[3 + a] - sigma * t[11 + a] for a in range(3)]
        c1 = at(0, 9)
        m1 = [at(0, 1) * inv, at(0, 2) * inv, at(0, 0)]
        qxx, qxy, qyy = at(0, 6) * inv2, at(0, 7) * inv2, at(0, 8) * inv2
        qx, qy, q1 = at(0, 4) * inv, at(0, 5) * inv, at(0, 3)
        q = [[qxx, qxy, qx], [qxy, qyy, qy], [qx, qy, q1]]
        p1 = [at(1 + d, 9) for d in range(3)]
        nd = [[at(1 + d, 1) * inv, at(1 + d, 2) * inv, at(1 + d, 0)] for d in range(3)]
        order = {}
        j = 0
        for a in range(3):
            for b in range(a, 3):
                order[(a, b)] = order[(b, a)] = j
                j += 1
        ppm = [[pp[order[(a, b)] : order[(a, b)] + 1, :] for b in range(3)] for a in range(3)]
        three = range(3)
        sturn = [[sigma * turn[a][d] for d in three] for a in three]
        s0 = [
            (sum(rot[a][j] * m1[j] for j in three) + tau[a] * c1 - sum(sturn[a][d] * p1[d] for d in three)) * live
            for a in three
        ]
        s1 = [
            [
                (sum(rot[a][l] * q[l][j] for l in three) + tau[a] * m1[j] - sum(sturn[a][d] * nd[d][j] for d in three)) * live
                for j in three
            ]
            for a in three
        ]
        s2 = [
            [
                (sum(rot[a][j] * nd[d][j] for j in three) + tau[a] * p1[d] - sum(sturn[a][b] * ppm[b][d] for b in three)) * live
                for d in three
            ]
            for a in three
        ]
        image_g = rotation_grad(t[0:3], rot, rot_s, s1) + s0
        image_g.append(-sum(rot[a][j] * s1[a][j] for a in three for j in range(2)))
        turn_g = [[-sigma * s2[a][d] for d in three] for a in three]
        pair_g = rotation_grad(t[8:11], turn, turn_s, turn_g) + [-sigma * s0[a] for a in three]
        pair_g.append(
            -sigma * (sum(turn[a][d] * s2[a][d] for a in three for d in three) + sum(t[11 + a] * s0[a] for a in three))
        )
        for i in range(7):
            term_ref[i : i + 1, :] = image_g[i]
            term_ref[8 + i : 9 + i, :] = pair_g[i]
        hot = hot_of()
        image_sum = nt(hot, term_ref[0:8, :], HIGH)
        join = (iota((24, TERMS), 0) == iota((24, TERMS), 1) // 2).astype(F32)
        pair_sum = nt(term_ref[8:16, :], join, HIGH)[0:7]
        new_p, new_m, new_v = adam(pp_ref[...], pair_sum, pm_ref[...], pv_ref[...], count_step)
        npp_ref[...] = new_p
        npm_ref[...] = new_m
        npv_ref[...] = new_v
        ip_ref[...] = jnp.zeros_like(ip_ref)
        ip_ref[:, 0:8] = image_sum
        pad = jnp.zeros((PROW - CHUNKS, 128), F32)
        for k in range(WIDTH):
            tail = jnp.where(iota((PROW - CHUNKS, 128), 0) == 0, ip_ref[k : k + 1, :], pad)
            outs[k][...] = jnp.concatenate([grad_ref[k * RS : k * RS + CHUNKS, :], tail], axis=0).astype(BF16)


def grads(count, bufs, crows, sums, sides_col, sides_row, live, pp, pm, pv):
    def whole(shape):
        return pl.BlockSpec(shape, lambda i: (0,) * len(shape))

    payload = whole((PROW, 128))
    pair = whole((7, 24))
    return pl.pallas_call(
        lambda *refs: grads_kernel(count, *refs),
        grid=(STEPS,),
        in_specs=[payload] * WIDTH
        + [
            pl.BlockSpec((CROWS, NB), lambda i: (0, i)),
            whole((TERMS, 128)),
            whole((TERMS, 1)),
            whole((1, TERMS)),
            pl.BlockSpec(memory_space=pltpu.SMEM),
            pair,
            pair,
            pair,
        ],
        out_specs=[payload] * WIDTH + [pair] * 3,
        out_shape=[jax.ShapeDtypeStruct((PROW, 128), BF16)] * WIDTH + [jax.ShapeDtypeStruct((7, 24), F32)] * 3,
        scratch_shapes=[
            pltpu.VMEM((WIDTH * RS, 128), F32),
            pltpu.VMEM((WIDTH * RS, 128), F32),
            pltpu.VMEM((128, CROWS), F32),
            pltpu.VMEM((CROWS, FCOLS), F32),
            pltpu.VMEM((16, 128), F32),
            pltpu.VMEM((16, TERMS), F32),
        ],
        compiler_params=pltpu.CompilerParams(vmem_limit_bytes=32 << 20),
        cost_estimate=pl.CostEstimate(flops=2_500_000_000, bytes_accessed=9_000_000, transcendentals=200_000),
        name="grads",
    )(*bufs, crows, sums, sides_col, sides_row, live, pp, pm, pv)


def on_device(
    log_depth, depth_m, depth_v, image_params, image_m, image_v,
    pair_points, pair_conf, pair_params, pair_m, pair_v, fetch, pair_sides, pair_count,
):
    devices_n = lax.axis_size("dev")
    offsets = [k - REACH for k in range(2 * REACH)] + [devices_n // 2]

    def shift(value, off):
        if off == 0:
            return value
        return lax.ppermute(value, "dev", [(i, (i + off) % devices_n) for i in range(devices_n)])

    served = [shift(fetch, off) for off in offsets]
    points = pair_points.transpose(2, 0, 1, 3).reshape(3, TERMS, PIX)
    conf = pair_conf.reshape(TERMS, PIX)
    crows, sums = prepare(points, conf)
    sides_row = pair_sides.reshape(1, TERMS)
    sides_col = pair_sides.reshape(TERMS, 1)

    def wide(value):
        return jnp.pad(value.T, ((0, 0), (0, 121)))

    ip, im, iv = wide(image_params), wide(image_m), wide(image_v)
    out = first(served, log_depth, ip)
    for step_id in range(ITERS):
        count = adam_start + step_id + 1
        last = step_id == ITERS - 1
        bufs = [shift(out[k], -offsets[k]) for k in range(WIDTH)]
        res = grads(count, bufs, crows, sums, sides_col, sides_row, pair_count, pair_params, pair_m, pair_v)
        back = [shift(res[k], offsets[k]) for k in range(WIDTH)]
        pair_params, pair_m, pair_v = res[WIDTH:]
        res = update(count, last, served, back, log_depth, depth_m, depth_v, ip, im, iv)
        if last:
            log_depth, ip = res
        else:
            log_depth, ip, depth_m, depth_v, im, iv = res[:6]
            out = res[6:]
    return (log_depth, ip[:, 0:7].T, pair_params)


def solution(mesh):
    return jax.shard_map(
        on_device,
        mesh=mesh,
        in_specs=(
            P("dev", None),
            P("dev", None),
            P("dev", None),
            P(None, "dev"),
            P(None, "dev"),
            P(None, "dev"),
            P("dev", None, None, None),
            P("dev", None, None),
            P(None, "dev"),
            P(None, "dev"),
            P(None, "dev"),
            P("dev", None),
            P("dev", None),
            P("dev"),
        ),
        out_specs=(P("dev", None), P(None, "dev"), P(None, "dev")),
        check_vma=False,
    )
```

```python
import jax
import jax.numpy as jnp
from jax import lax
from jax.experimental import pallas as pl
from jax.experimental.pallas import tpu as pltpu
from jax.sharding import PartitionSpec as P

IMG_SIDE = 112
PIX = 12544
REACH = 4
ITERS = 2
WIDTH = 2 * REACH + 1
CHUNKS = PIX // 128
PROW = 112
RS = 104
NB = 1792
STEPS = PIX // NB
SUB = NB // 128
SLOTS = 24
TERMS = 2 * SLOTS
CROWS = 7 * TERMS
FCOLS = 176

focal_base = 100.0
learn_rate = 0.05
beta_one = 0.9
beta_two = 0.999
adam_epsilon = 1e-08
adam_start = 20


F32 = jnp.float32
BF16 = jnp.bfloat16
HIGH = lax.Precision.HIGHEST


def adam(param, grad, moment, second, count):
    moment = beta_one * moment + (1.0 - beta_one) * grad
    second = beta_two * second + (1.0 - beta_two) * grad * grad
    fix_one = 1.0 - beta_one**count
    fix_two = 1.0 - beta_two**count
    step = (learn_rate / fix_one) * moment / (jnp.sqrt(second * (1.0 / fix_two)) + adam_epsilon)
    return param - step, moment, second


def rotation(vec):
    x, y, z = vec
    s = 1.0 / (1.0 + x * x + y * y + z * z)
    return [
        [(1.0 + x * x - y * y - z * z) * s, 2.0 * (x * y - z) * s, 2.0 * (x * z + y) * s],
        [2.0 * (x * y + z) * s, (1.0 - x * x + y * y - z * z) * s, 2.0 * (y * z - x) * s],
        [2.0 * (x * z - y) * s, 2.0 * (y * z + x) * s, (1.0 - x * x - y * y + z * z) * s],
    ], s


def rotation_grad(vec, rot, s, g):
    x, y, z = vec
    inner = sum(g[i][j] * rot[i][j] for i in range(3) for j in range(3))
    s2 = 2.0 * s
    gx = x * (g[0][0] - g[1][1] - g[2][2]) + y * (g[0][1] + g[1][0]) + z * (g[0][2] + g[2][0]) + (g[2][1] - g[1][2])
    gy = y * (g[1][1] - g[0][0] - g[2][2]) + x * (g[0][1] + g[1][0]) + z * (g[1][2] + g[2][1]) + (g[0][2] - g[2][0])
    gz = z * (g[2][2] - g[0][0] - g[1][1]) + x * (g[0][2] + g[2][0]) + y * (g[1][2] + g[2][1]) + (g[1][0] - g[0][1])
    return [s2 * (gx - x * inner), s2 * (gy - y * inner), s2 * (gz - z * inner)]


def split(value):
    high = value.astype(BF16).astype(F32)
    return high, value - high


def nt(lhs, rhs, precision=None):
    return lax.dot_general(lhs, rhs, (((1,), (1,)), ((), ())), precision=precision, preferred_element_type=F32)


def nn(lhs, rhs, precision=None):
    return lax.dot_general(lhs, rhs, (((1,), (0,)), ((), ())), precision=precision, preferred_element_type=F32)


def iota(shape, dim):
    return lax.broadcasted_iota(jnp.int32, shape, dim)


def prepare_kernel(points_ref, conf_ref, out_ref, sums_ref, acc_ref):
    step = pl.program_id(0)

    @pl.when(step == 0)
    def _():
        acc_ref[...] = jnp.zeros_like(acc_ref)

    conf = conf_ref[...].astype(F32).reshape(TERMS, NB).astype(BF16)
    out_ref[0:TERMS, :] = conf
    conf = conf.astype(F32)
    pts = []
    for d in range(3):
        rows = points_ref[:, d].astype(F32).reshape(TERMS, NB).astype(BF16)
        out_ref[(1 + d) * TERMS : (2 + d) * TERMS, :] = rows
        pts.append(rows.astype(F32))
    weighted = [conf * pts[d] for d in range(3)]
    j = 0
    for a in range(3):
        for b in range(a, 3):
            prod = weighted[a] * pts[b]
            total = prod[:, 0:128]
            for c in range(1, SUB):
                total = total + prod[:, c * 128 : (c + 1) * 128]
            acc_ref[j] += total
            j += 1

    @pl.when(step == STEPS - 1)
    def _():
        lane = iota((TERMS, 128), 1)
        res = jnp.zeros((TERMS, 128), F32)
        for i in range(6):
            res = jnp.where(lane == i, jnp.sum(acc_ref[i], axis=1, keepdims=True), res)
        sums_ref[...] = res


def prepare(points, conf):
    return pl.pallas_call(
        prepare_kernel,
        grid=(STEPS,),
        in_specs=[
            pl.BlockSpec((SLOTS, 3, 2, NB), lambda i: (0, 0, 0, i)),
            pl.BlockSpec((SLOTS, 2, NB), lambda i: (0, 0, i)),
        ],
        out_specs=[
            pl.BlockSpec((4 * TERMS, NB), lambda i: (0, i)),
            pl.BlockSpec((TERMS, 128), lambda i: (0, 0)),
        ],
        out_shape=[
            pltpu.HBM((4 * TERMS, PIX), BF16),
            jax.ShapeDtypeStruct((TERMS, 128), F32),
        ],
        scratch_shapes=[pltpu.VMEM((6, TERMS, 128), F32)],
        compiler_params=pltpu.CompilerParams(vmem_limit_bytes=16 << 20),
        cost_estimate=pl.CostEstimate(flops=20_000_000, bytes_accessed=14_000_000, transcendentals=0),
        name="prepare",
    )(points, conf)


def pick_payloads(served, rows_ref, param_rows, out_refs):
    pad = jnp.zeros((PROW - CHUNKS, 128), F32)
    for k in range(WIDTH):
        image = served[k]
        pixels = rows_ref[pl.ds(image, CHUNKS, stride=8), :]
        row = param_rows[pl.ds(image, 1), :]
        tail = jnp.where(iota((PROW - CHUNKS, 128), 0) == 0, row, pad)
        out_refs[k][...] = jnp.concatenate([pixels, tail], axis=0).astype(BF16)


def first_kernel(got_ref, depth_ref, param_ref, after_ref, *refs):
    del after_ref
    outs = refs[:WIDTH]
    served_ref, rows_ref, asked_ref, sems = refs[WIDTH:]
    devices_n = got_ref.shape[0]
    me = lax.axis_index("dev")
    copies = []
    for k in range(WIDTH):
        off = k - REACH if k < 2 * REACH else devices_n // 2
        holder = lax.rem(me - off + devices_n, devices_n)
        copies.append(pltpu.make_async_copy(got_ref.at[holder], asked_ref.at[k], sems.at[k]))
        copies[k].start()
    for c in range(CHUNKS):
        rows_ref[8 * c : 8 * c + 8, :] = depth_ref[:, 128 * c : 128 * c + 128]
    served = []
    for k in range(WIDTH):
        copies[k].wait()
        served.append(asked_ref[k, 0, k])
        served_ref[0, k] = served[k]
    pick_payloads(served, rows_ref, param_ref, outs)


def first(got, depth, params, after):
    sm = pl.BlockSpec(memory_space=pltpu.SMEM)
    vm = pl.BlockSpec(memory_space=pltpu.VMEM)
    return pl.pallas_call(
        first_kernel,
        in_specs=[pl.BlockSpec(memory_space=pl.ANY), vm, vm, vm],
        out_specs=[vm] * WIDTH + [sm],
        out_shape=[jax.ShapeDtypeStruct((PROW, 128), BF16)] * WIDTH + [jax.ShapeDtypeStruct((1, WIDTH), jnp.int32)],
        scratch_shapes=[
            pltpu.VMEM((8 * CHUNKS, 128), F32),
            pltpu.SMEM((WIDTH, 1, WIDTH), jnp.int32),
            pltpu.SemaphoreType.DMA((WIDTH,)),
        ],
        compiler_params=pltpu.CompilerParams(vmem_limit_bytes=8 << 20),
        cost_estimate=pl.CostEstimate(flops=1_000_000, bytes_accessed=700_000, transcendentals=0),
        name="first",
    )(got, depth, params, after)


def update_kernel(count, last, *refs):
    served = [refs[0][0, k] for k in range(WIDTH)]
    back = refs[1 : WIDTH + 1]
    depth_ref, m_ref, v_ref, ip_ref, im_ref, iv_ref = refs[WIDTH + 1 : WIDTH + 7]
    rest = refs[WIDTH + 7 :]
    n_out = 2 if last else 6 + WIDTH
    outs = rest[:n_out]
    acc_ref, pacc_ref = rest[n_out : n_out + 2]
    acc_ref[...] = jnp.zeros_like(acc_ref)
    pacc_ref[...] = jnp.zeros_like(pacc_ref)
    for k in range(WIDTH):
        image = served[k]
        value = back[k][...].astype(F32)
        where = pl.ds(image, CHUNKS, stride=8)
        acc_ref[where, :] = acc_ref[where, :] + value[0:CHUNKS]
        pacc_ref[pl.ds(image, 1), :] = pacc_ref[pl.ds(image, 1), :] + value[CHUNKS : CHUNKS + 1]
    for c in range(CHUNKS):
        cols = slice(128 * c, 128 * c + 128)
        rows = slice(8 * c, 8 * c + 8)
        depth, m, v = adam(depth_ref[:, cols], acc_ref[rows, :], m_ref[:, cols], v_ref[:, cols], count)
        outs[0][:, cols] = depth
        if not last:
            outs[2][:, cols] = m
            outs[3][:, cols] = v
            acc_ref[rows, :] = depth
    param, pm, pv = adam(ip_ref[...], pacc_ref[...], im_ref[...], iv_ref[...], count)
    outs[1][...] = param
    if not last:
        outs[4][...] = pm
        outs[5][...] = pv
        pick_payloads(served, acc_ref, outs[1], outs[6:])


def update(count, last, served, back, depth, m, v, ip, im, iv):
    big = jax.ShapeDtypeStruct((8, PIX), F32)
    small = jax.ShapeDtypeStruct((8, 128), F32)
    shapes = [big, small] if last else [big, small, big, big, small, small] + [jax.ShapeDtypeStruct((PROW, 128), BF16)] * WIDTH
    vm = pl.BlockSpec(memory_space=pltpu.VMEM)
    return pl.pallas_call(
        lambda *refs: update_kernel(count, last, *refs),
        in_specs=[pl.BlockSpec(memory_space=pltpu.SMEM)] + [vm] * (WIDTH + 6),
        out_specs=[vm] * len(shapes),
        out_shape=shapes,
        scratch_shapes=[pltpu.VMEM((8 * CHUNKS, 128), F32), pltpu.VMEM((8, 128), F32)],
        compiler_params=pltpu.CompilerParams(vmem_limit_bytes=8 << 20),
        cost_estimate=pl.CostEstimate(flops=3_000_000, bytes_accessed=2_500_000, transcendentals=0),
        name="update",
    )(served, *back, depth, m, v, ip, im, iv)


def grads_kernel(count_step, *refs):
    bufs = refs[:WIDTH]
    crows_ref, sums_ref, sides_col_ref, sides_row_ref, live_ref, pp_ref, pm_ref, pv_ref = refs[WIDTH : WIDTH + 8]
    outs = refs[WIDTH + 8 : 2 * WIDTH + 8]
    npp_ref, npm_ref, npv_ref = refs[2 * WIDTH + 8 : 2 * WIDTH + 11]
    depth_ref, grad_ref, coef_ref, mom_ref, ip_ref, term_ref, blocks_ref, sems = refs[2 * WIDTH + 11 :]
    kappa = 2.0 / PIX

    def fetch(step):
        cols = pl.ds(pl.multiple_of(step * NB, 128), NB)
        return pltpu.make_async_copy(crows_ref.at[:, cols], blocks_ref.at[step], sems.at[step])

    for step in range(STEPS):
        fetch(step).start()

    def hot_of():
        return (iota((16, TERMS), 0) == sides_row_ref[...]).astype(F32)

    def term_rows():
        return [term_ref[i : i + 1, :] for i in range(16)]

    ip_ref[...] = jnp.zeros_like(ip_ref)
    for k in range(WIDTH):
        value = bufs[k][...].astype(F32)
        depth_ref[k * RS : k * RS + CHUNKS, :] = value[0:CHUNKS]
        ip_ref[k : k + 1, :] = value[CHUNKS : CHUNKS + 1]
    mom_ref[...] = jnp.zeros_like(mom_ref)
    hot = hot_of()
    images = lax.dot_general(ip_ref[...], hot, (((0,), (0,)), ((), ())), precision=HIGH, preferred_element_type=F32)
    spread = (iota((24, TERMS), 0) == iota((24, TERMS), 1) // 2).astype(F32)
    pairs = nn(pp_ref[...], spread, HIGH)
    term_ref[0:8, :] = images[0:8, :]
    term_ref[8:15, :] = pairs
    t = term_rows()
    rot, _ = rotation(t[0:3])
    turn, _ = rotation(t[8:11])
    sigma = jnp.exp(t[14])
    live = (iota((1, TERMS), 1) // 2 < live_ref[0]).astype(F32) * kappa
    tau = [t[3 + a] - sigma * t[11 + a] for a in range(3)]
    zero = jnp.zeros((16, TERMS), F32)
    blocks = []
    for j in range(3):
        a_j = (rot[0][j] * tau[0] + rot[1][j] * tau[1] + rot[2][j] * tau[2]) * live
        b_j = [
            -(rot[0][j] * turn[0][d] + rot[1][j] * turn[1][d] + rot[2][j] * turn[2][d]) * sigma * live
            for d in range(3)
        ]
        blocks.append([hot * a_j] + [hot * b for b in b_j])
    blocks.append([hot * live, zero, zero, zero])
    for j in range(4):
        for n in range(4):
            high, low = split(blocks[j][n])
            for where in ([n] if n == 0 else [n, n + 3]):
                coef_ref[16 * j : 16 * j + 16, where * TERMS : (where + 1) * TERMS] = high
                coef_ref[64 + 16 * j : 80 + 16 * j, where * TERMS : (where + 1) * TERMS] = low

    def block(step, carry):
        fetch(step).wait()
        pos = (iota((8, NB), 1) + step * NB).astype(F32)
        row = jnp.floor((pos + 0.5) * (1.0 / IMG_SIDE))
        x = pos - row * IMG_SIDE - (IMG_SIDE - 1) / 2.0
        y = row - (IMG_SIDE - 1) / 2.0
        near = jnp.concatenate([depth_ref[pl.ds(step * SUB + c, 8, stride=RS), :] for c in range(SUB)], axis=1)
        far = jnp.concatenate([depth_ref[pl.ds(8 * RS + step * SUB + c, 1), :] for c in range(SUB)], axis=1)
        near = jnp.exp(near)
        far = jnp.exp(far)
        near2 = near * near
        fields = [near, near * x, near * y, near2, near2 * x, near2 * y]
        fields += [fields[4] * x, fields[4] * y, fields[5] * y]
        sub = iota((8, NB), 0)
        farb = jnp.broadcast_to(far, (8, NB))
        base = jnp.where(sub < 3, farb, farb * farb)
        first_w = jnp.where((sub == 1) | (sub == 4), x, jnp.where((sub == 2) | (sub == 5), y, 1.0))
        first_w = jnp.where(sub >= 6, x, first_w)
        second_w = jnp.where(sub == 6, x, jnp.where(sub == 7, y, 1.0))
        fields.append(base * first_w * second_w)
        fields.append(jnp.where(sub == 0, farb * farb * y * y, jnp.where(sub == 1, 1.0, 0.0)))
        tiles = []
        for value in fields:
            high, low = split(value)
            tiles.append(jnp.concatenate([high, low], axis=0).astype(BF16))
        stack = jnp.concatenate(tiles, axis=0)
        conf = blocks_ref[step, 0:TERMS, :]
        conf_wide = conf.astype(F32)
        highs = []
        lows = []
        for d in range(3):
            high, low = split(conf_wide * blocks_ref[step, (1 + d) * TERMS : (2 + d) * TERMS, :].astype(F32))
            highs.append(high.astype(BF16))
            lows.append(low.astype(BF16))
        crows = jnp.concatenate([conf] + highs + lows, axis=0)
        mom_ref[...] += nt(crows, stack)

        out = nn(coef_ref[...].astype(BF16), crows)
        out = out[0:64] + out[64:128]
        inv_f = 1.0 / (focal_base * jnp.exp(ip_ref[:, 6:7]))
        near_f = inv_f[0:8]
        far_f = inv_f[8:9]
        rr = x * x + y * y
        near_g = near * (near * (rr * (near_f * near_f) + 1.0) * out[48:56] + (x * out[0:8] + y * out[16:24]) * near_f + out[32:40])
        far_g = far * (
            far * (rr[0:1] * (far_f * far_f) + 1.0) * out[56:57] + (x[0:1] * out[8:9] + y[0:1] * out[24:25]) * far_f + out[40:41]
        )
        for c in range(SUB):
            grad_ref[pl.ds(step * SUB + c, 8, stride=RS), :] = near_g[:, 128 * c : 128 * c + 128]
            grad_ref[pl.ds(8 * RS + step * SUB + c, 1), :] = far_g[:, 128 * c : 128 * c + 128]
        return carry

    lax.fori_loop(0, STEPS, block, 0)

    col = iota((TERMS, FCOLS), 1)
    image_of = jnp.where(col < 144, col % 8, 8)
    mask = ((image_of == sides_col_ref[...]) | (col == 161)).astype(F32)
    fcol = iota((16, FCOLS), 1)
    inside = jnp.where(
        fcol < 144,
        fcol // 16,
        jnp.where(fcol < 160, fcol % 8, jnp.where(fcol % 8 == 0, 8, jnp.where(fcol == 161, 9, 20))),
    )
    pickf = (inside == iota((16, FCOLS), 0)).astype(F32)
    groups = [nt(pickf, mom_ref[0:TERMS, :] * mask, HIGH)]
    for d in range(3):
        both = mom_ref[(1 + d) * TERMS : (2 + d) * TERMS, :] + mom_ref[(4 + d) * TERMS : (5 + d) * TERMS, :]
        groups.append(nt(pickf, both * mask, HIGH))
    eye = (iota((8, 128), 0) == iota((8, 128), 1)).astype(F32)
    pp = nt(eye, sums_ref[...], HIGH)

    def at(group, field):
        return groups[group][field : field + 1, :]

    t = term_rows()
    rot, rot_s = rotation(t[0:3])
    turn, turn_s = rotation(t[8:11])
    sigma = jnp.exp(t[14])
    inv = 1.0 / (focal_base * jnp.exp(t[6]))
    inv2 = inv * inv
    live = (iota((1, TERMS), 1) // 2 < live_ref[0]).astype(F32) * kappa
    tau = [t[3 + a] - sigma * t[11 + a] for a in range(3)]
    c1 = at(0, 9)
    m1 = [at(0, 1) * inv, at(0, 2) * inv, at(0, 0)]
    qxx, qxy, qyy = at(0, 6) * inv2, at(0, 7) * inv2, at(0, 8) * inv2
    qx, qy, q1 = at(0, 4) * inv, at(0, 5) * inv, at(0, 3)
    q = [[qxx, qxy, qx], [qxy, qyy, qy], [qx, qy, q1]]
    p1 = [at(1 + d, 9) for d in range(3)]
    nd = [[at(1 + d, 1) * inv, at(1 + d, 2) * inv, at(1 + d, 0)] for d in range(3)]
    order = {}
    j = 0
    for a in range(3):
        for b in range(a, 3):
            order[(a, b)] = order[(b, a)] = j
            j += 1
    ppm = [[pp[order[(a, b)] : order[(a, b)] + 1, :] for b in range(3)] for a in range(3)]
    three = range(3)
    sturn = [[sigma * turn[a][d] for d in three] for a in three]
    s0 = [
        (sum(rot[a][j] * m1[j] for j in three) + tau[a] * c1 - sum(sturn[a][d] * p1[d] for d in three)) * live
        for a in three
    ]
    s1 = [
        [
            (sum(rot[a][l] * q[l][j] for l in three) + tau[a] * m1[j] - sum(sturn[a][d] * nd[d][j] for d in three)) * live
            for j in three
        ]
        for a in three
    ]
    s2 = [
        [
            (sum(rot[a][j] * nd[d][j] for j in three) + tau[a] * p1[d] - sum(sturn[a][b] * ppm[b][d] for b in three)) * live
            for d in three
        ]
        for a in three
    ]
    image_g = rotation_grad(t[0:3], rot, rot_s, s1) + s0
    image_g.append(-sum(rot[a][j] * s1[a][j] for a in three for j in range(2)))
    turn_g = [[-sigma * s2[a][d] for d in three] for a in three]
    pair_g = rotation_grad(t[8:11], turn, turn_s, turn_g) + [-sigma * s0[a] for a in three]
    pair_g.append(
        -sigma * (sum(turn[a][d] * s2[a][d] for a in three for d in three) + sum(t[11 + a] * s0[a] for a in three))
    )
    for i in range(7):
        term_ref[i : i + 1, :] = image_g[i]
        term_ref[8 + i : 9 + i, :] = pair_g[i]
    hot = hot_of()
    image_sum = nt(hot, term_ref[0:8, :], HIGH)
    join = (iota((24, TERMS), 0) == iota((24, TERMS), 1) // 2).astype(F32)
    pair_sum = nt(term_ref[8:16, :], join, HIGH)[0:7]
    new_p, new_m, new_v = adam(pp_ref[...], pair_sum, pm_ref[...], pv_ref[...], count_step)
    npp_ref[...] = new_p
    npm_ref[...] = new_m
    npv_ref[...] = new_v
    ip_ref[...] = jnp.zeros_like(ip_ref)
    ip_ref[:, 0:8] = image_sum
    pad = jnp.zeros((PROW - CHUNKS, 128), F32)
    for k in range(WIDTH):
        tail = jnp.where(iota((PROW - CHUNKS, 128), 0) == 0, ip_ref[k : k + 1, :], pad)
        outs[k][...] = jnp.concatenate([grad_ref[k * RS : k * RS + CHUNKS, :], tail], axis=0).astype(BF16)


def grads(count, bufs, crows, sums, sides_col, sides_row, live, pp, pm, pv):
    payload = pair = vm = pl.BlockSpec(memory_space=pltpu.VMEM)
    return pl.pallas_call(
        lambda *refs: grads_kernel(count, *refs),
        in_specs=[payload] * WIDTH
        + [
            pl.BlockSpec(memory_space=pltpu.HBM),
            vm,
            vm,
            vm,
            pl.BlockSpec(memory_space=pltpu.SMEM),
            pair,
            pair,
            pair,
        ],
        out_specs=[payload] * WIDTH + [pair] * 3,
        out_shape=[jax.ShapeDtypeStruct((PROW, 128), BF16)] * WIDTH + [jax.ShapeDtypeStruct((7, 24), F32)] * 3,
        scratch_shapes=[
            pltpu.VMEM((WIDTH * RS, 128), F32),
            pltpu.VMEM((WIDTH * RS, 128), F32),
            pltpu.VMEM((128, CROWS), F32),
            pltpu.VMEM((CROWS, FCOLS), F32),
            pltpu.VMEM((16, 128), F32),
            pltpu.VMEM((16, TERMS), F32),
            pltpu.VMEM((STEPS, 4 * TERMS, NB), BF16),
            pltpu.SemaphoreType.DMA((STEPS,)),
        ],
        compiler_params=pltpu.CompilerParams(vmem_limit_bytes=20 << 20),
        cost_estimate=pl.CostEstimate(flops=2_500_000_000, bytes_accessed=9_000_000, transcendentals=200_000),
        name="grads",
    )(*bufs, crows, sums, sides_col, sides_row, live, pp, pm, pv)


def on_device(
    log_depth, depth_m, depth_v, image_params, image_m, image_v,
    pair_points, pair_conf, pair_params, pair_m, pair_v, fetch, pair_sides, pair_count,
):
    devices_n = lax.axis_size("dev")
    offsets = [k - REACH for k in range(2 * REACH)] + [devices_n // 2]

    def shift(value, off):
        if off == 0:
            return value
        return lax.ppermute(value, "dev", [(i, (i + off) % devices_n) for i in range(devices_n)])

    asked = jnp.broadcast_to(fetch[:, None, :], (devices_n, 1, WIDTH))
    got = lax.all_to_all(asked, "dev", split_axis=0, concat_axis=0, tiled=True)
    points = pltpu.with_memory_space_constraint(pair_points.transpose(0, 2, 1, 3), pltpu.HBM)
    crows, sums = prepare(points, pltpu.with_memory_space_constraint(pair_conf, pltpu.HBM))
    sides_row = pair_sides.reshape(1, TERMS)
    sides_col = pair_sides.reshape(TERMS, 1)

    def wide(value):
        return jnp.pad(value.T, ((0, 0), (0, 121)))

    ip, im, iv = wide(image_params), wide(image_m), wide(image_v)
    res = first(got, log_depth, ip, sums)
    out, served = res[:WIDTH], res[WIDTH]
    for step_id in range(ITERS):
        count = adam_start + step_id + 1
        last = step_id == ITERS - 1
        bufs = [shift(out[k], -offsets[k]) for k in range(WIDTH)]
        res = grads(count, bufs, pltpu.with_memory_space_constraint(crows, pltpu.HBM), sums, sides_col, sides_row, pair_count, pair_params, pair_m, pair_v)
        back = [shift(res[k], offsets[k]) for k in range(WIDTH)]
        pair_params, pair_m, pair_v = res[WIDTH:]
        res = update(count, last, served, back, log_depth, depth_m, depth_v, ip, im, iv)
        if last:
            log_depth, ip = res
        else:
            log_depth, ip, depth_m, depth_v, im, iv = res[:6]
            out = res[6:]
    return (log_depth, ip[:, 0:7].T, pair_params)


def solution(mesh):
    return jax.shard_map(
        on_device,
        mesh=mesh,
        in_specs=(
            P("dev", None),
            P("dev", None),
            P("dev", None),
            P(None, "dev"),
            P(None, "dev"),
            P(None, "dev"),
            P("dev", None, None, None),
            P("dev", None, None),
            P(None, "dev"),
            P(None, "dev"),
            P(None, "dev"),
            P("dev", None),
            P("dev", None),
            P("dev"),
        ),
        out_specs=(P("dev", None), P(None, "dev"), P(None, "dev")),
        check_vma=False,
    )
```

```python
import jax
import jax.numpy as jnp
from jax import lax
from jax.experimental import pallas as pl
from jax.experimental.pallas import tpu as pltpu
from jax.sharding import PartitionSpec as P

IMG_SIDE = 112
PIX = 12544
REACH = 4
ITERS = 2
WIDTH = 2 * REACH + 1
CHUNKS = PIX // 128
PROW = 104
ASK = 8
RS = 104
NB = 1792
STEPS = PIX // NB
SUB = NB // 128
SLOTS = 24
TERMS = 2 * SLOTS
CROWS = 7 * TERMS
FCOLS = 176

focal_base = 100.0
learn_rate = 0.05
beta_one = 0.9
beta_two = 0.999
adam_epsilon = 1e-08
adam_start = 20


CHIPS = (-2, -1, 1, 2)

F32 = jnp.float32
BF16 = jnp.bfloat16
HIGH = lax.Precision.HIGHEST


def adam(param, grad, moment, second, count):
    moment = beta_one * moment + (1.0 - beta_one) * grad
    second = beta_two * second + (1.0 - beta_two) * grad * grad
    fix_one = 1.0 - beta_one**count
    fix_two = 1.0 - beta_two**count
    step = (learn_rate / fix_one) * moment / (jnp.sqrt(second * (1.0 / fix_two)) + adam_epsilon)
    return param - step, moment, second


def rotation(vec):
    x, y, z = vec
    s = 1.0 / (1.0 + x * x + y * y + z * z)
    return [
        [(1.0 + x * x - y * y - z * z) * s, 2.0 * (x * y - z) * s, 2.0 * (x * z + y) * s],
        [2.0 * (x * y + z) * s, (1.0 - x * x + y * y - z * z) * s, 2.0 * (y * z - x) * s],
        [2.0 * (x * z - y) * s, 2.0 * (y * z + x) * s, (1.0 - x * x - y * y + z * z) * s],
    ], s


def rotation_grad(vec, rot, s, g):
    x, y, z = vec
    inner = sum(g[i][j] * rot[i][j] for i in range(3) for j in range(3))
    s2 = 2.0 * s
    gx = x * (g[0][0] - g[1][1] - g[2][2]) + y * (g[0][1] + g[1][0]) + z * (g[0][2] + g[2][0]) + (g[2][1] - g[1][2])
    gy = y * (g[1][1] - g[0][0] - g[2][2]) + x * (g[0][1] + g[1][0]) + z * (g[1][2] + g[2][1]) + (g[0][2] - g[2][0])
    gz = z * (g[2][2] - g[0][0] - g[1][1]) + x * (g[0][2] + g[2][0]) + y * (g[1][2] + g[2][1]) + (g[1][0] - g[0][1])
    return [s2 * (gx - x * inner), s2 * (gy - y * inner), s2 * (gz - z * inner)]


def split(value):
    high = value.astype(BF16).astype(F32)
    return high, value - high


def nt(lhs, rhs, precision=None):
    return lax.dot_general(lhs, rhs, (((1,), (1,)), ((), ())), precision=precision, preferred_element_type=F32)


def nn(lhs, rhs, precision=None):
    return lax.dot_general(lhs, rhs, (((1,), (0,)), ((), ())), precision=precision, preferred_element_type=F32)


def iota(shape, dim):
    return lax.broadcasted_iota(jnp.int32, shape, dim)


def prepare_kernel(points_ref, conf_ref, out_ref, sums_ref, acc_ref):
    step = pl.program_id(0)

    @pl.when(step == 0)
    def _():
        acc_ref[...] = jnp.zeros_like(acc_ref)

    conf = conf_ref[...].astype(F32).reshape(TERMS, NB).astype(BF16)
    out_ref[0:TERMS, :] = conf
    conf = conf.astype(F32)
    pts = []
    for d in range(3):
        rows = points_ref[:, d].astype(F32).reshape(TERMS, NB).astype(BF16)
        out_ref[(1 + d) * TERMS : (2 + d) * TERMS, :] = rows
        pts.append(rows.astype(F32))
    weighted = [conf * pts[d] for d in range(3)]
    j = 0
    for a in range(3):
        for b in range(a, 3):
            prod = weighted[a] * pts[b]
            total = prod[:, 0:128]
            for c in range(1, SUB):
                total = total + prod[:, c * 128 : (c + 1) * 128]
            acc_ref[j] += total
            j += 1

    @pl.when(step == STEPS - 1)
    def _():
        lane = iota((TERMS, 128), 1)
        res = jnp.zeros((TERMS, 128), F32)
        for i in range(6):
            res = jnp.where(lane == i, jnp.sum(acc_ref[i], axis=1, keepdims=True), res)
        sums_ref[...] = res


def prepare(points, conf):
    return pl.pallas_call(
        prepare_kernel,
        grid=(STEPS,),
        in_specs=[
            pl.BlockSpec((SLOTS, 3, 2, NB), lambda i: (0, 0, 0, i)),
            pl.BlockSpec((SLOTS, 2, NB), lambda i: (0, 0, i)),
        ],
        out_specs=[
            pl.BlockSpec((4 * TERMS, NB), lambda i: (0, i)),
            pl.BlockSpec((TERMS, 128), lambda i: (0, 0)),
        ],
        out_shape=[
            pltpu.HBM((4 * TERMS, PIX), BF16),
            jax.ShapeDtypeStruct((TERMS, 128), F32),
        ],
        scratch_shapes=[pltpu.VMEM((6, TERMS, 128), F32)],
        compiler_params=pltpu.CompilerParams(vmem_limit_bytes=16 << 20),
        cost_estimate=pl.CostEstimate(flops=20_000_000, bytes_accessed=14_000_000, transcendentals=0),
        name="prepare",
    )(points, conf)


def payload_of(rows_ref, param_rows, image):
    pixels = rows_ref[pl.ds(image, CHUNKS, stride=8), :]
    row = param_rows[pl.ds(image, 1), :]
    tail = jnp.where(iota((PROW - CHUNKS, 128), 0) == 0, row, 0.0)
    return jnp.concatenate([pixels, tail], axis=0).astype(BF16)


def pack_kernel(depth_ref, param_ref, out_ref, rows_ref):
    for c in range(CHUNKS):
        rows_ref[8 * c : 8 * c + 8, :] = depth_ref[:, 128 * c : 128 * c + 128]
    for image in range(8):
        out_ref[image] = payload_of(rows_ref, param_ref, image)


def pack(depth, params):
    vm = pl.BlockSpec(memory_space=pltpu.VMEM)
    return pl.pallas_call(
        pack_kernel,
        in_specs=[vm, vm],
        out_specs=vm,
        out_shape=jax.ShapeDtypeStruct((8, PROW, 128), BF16),
        scratch_shapes=[pltpu.VMEM((8 * CHUNKS, 128), F32)],
        compiler_params=pltpu.CompilerParams(vmem_limit_bytes=8 << 20),
        cost_estimate=pl.CostEstimate(flops=1_000_000, bytes_accessed=700_000, transcendentals=0),
        name="pack",
    )(depth, params)


def forward_kernel(ask_ref, after_ref, *refs):
    del after_ref
    bufs = refs[: len(CHIPS)]
    out_ref = refs[len(CHIPS)]
    side = 1 - 2 * lax.rem(lax.axis_index("dev"), 2)
    for i, chip in enumerate(CHIPS):
        k = jnp.clip(REACH + 2 * chip - side, 0, 2 * REACH - 1)
        out_ref[i] = bufs[i][ask_ref[0, k]]


def forward(ask, after, bufs):
    vm = pl.BlockSpec(memory_space=pltpu.VMEM)
    return pl.pallas_call(
        forward_kernel,
        in_specs=[pl.BlockSpec(memory_space=pltpu.SMEM)] + [vm] * (len(CHIPS) + 1),
        out_specs=vm,
        out_shape=jax.ShapeDtypeStruct((len(CHIPS), PROW, 128), BF16),
        compiler_params=pltpu.CompilerParams(vmem_limit_bytes=4 << 20),
        cost_estimate=pl.CostEstimate(flops=1_000, bytes_accessed=230_000, transcendentals=0),
        name="forward",
    )(ask, after, *bufs)


def update_kernel(count, last, *refs):
    back = refs[:WIDTH]
    depth_ref, m_ref, v_ref, ip_ref, im_ref, iv_ref = refs[WIDTH : WIDTH + 6]
    rest = refs[WIDTH + 6 :]
    n_out = 2 if last else 6 + WIDTH
    outs = rest[:n_out]
    acc_ref, pacc_ref = rest[n_out : n_out + 2]
    acc_ref[...] = jnp.zeros_like(acc_ref)
    pacc_ref[...] = jnp.zeros_like(pacc_ref)
    lane = iota((1, 128), 1)
    served = []
    for k in range(WIDTH):
        row = back[k][CHUNKS:PROW, :].astype(F32)[0:1]
        served.append(jnp.sum(jnp.where(lane == ASK, row, 0.0)).astype(jnp.int32))
    for k in range(WIDTH):
        image = served[k]
        value = back[k][...].astype(F32)
        where = pl.ds(image, CHUNKS, stride=8)
        acc_ref[where, :] = acc_ref[where, :] + value[0:CHUNKS]
        row = jnp.where(lane < ASK, value[CHUNKS : CHUNKS + 1], 0.0)
        pacc_ref[pl.ds(image, 1), :] = pacc_ref[pl.ds(image, 1), :] + row
    for c in range(CHUNKS):
        cols = slice(128 * c, 128 * c + 128)
        rows = slice(8 * c, 8 * c + 8)
        depth, m, v = adam(depth_ref[:, cols], acc_ref[rows, :], m_ref[:, cols], v_ref[:, cols], count)
        outs[0][:, cols] = depth
        if not last:
            outs[2][:, cols] = m
            outs[3][:, cols] = v
            acc_ref[rows, :] = depth
    param, pm, pv = adam(ip_ref[...], pacc_ref[...], im_ref[...], iv_ref[...], count)
    outs[1][...] = param
    if not last:
        outs[4][...] = pm
        outs[5][...] = pv
        for k in range(WIDTH):
            outs[6 + k][...] = payload_of(acc_ref, outs[1], served[k])


def update(count, last, back, depth, m, v, ip, im, iv):
    big = jax.ShapeDtypeStruct((8, PIX), F32)
    small = jax.ShapeDtypeStruct((8, 128), F32)
    shapes = [big, small] if last else [big, small, big, big, small, small] + [jax.ShapeDtypeStruct((PROW, 128), BF16)] * WIDTH
    vm = pl.BlockSpec(memory_space=pltpu.VMEM)
    return pl.pallas_call(
        lambda *refs: update_kernel(count, last, *refs),
        in_specs=[vm] * (WIDTH + 6),
        out_specs=[vm] * len(shapes),
        out_shape=shapes,
        scratch_shapes=[pltpu.VMEM((8 * CHUNKS, 128), F32), pltpu.VMEM((8, 128), F32)],
        compiler_params=pltpu.CompilerParams(vmem_limit_bytes=8 << 20),
        cost_estimate=pl.CostEstimate(flops=3_000_000, bytes_accessed=2_500_000, transcendentals=0),
        name="update",
    )(*back, depth, m, v, ip, im, iv)


def grads_kernel(count_step, pick, fetch_ref, *refs):
    n_in = 4 + len([c for c in CHIPS if 2 * c < REACH]) if pick else WIDTH
    bufs = refs[:n_in]
    crows_ref, sums_ref, sides_col_ref, sides_row_ref, live_ref, pp_ref, pm_ref, pv_ref = refs[n_in : n_in + 8]
    outs = refs[n_in + 8 : n_in + 8 + WIDTH]
    npp_ref, npm_ref, npv_ref = refs[n_in + 8 + WIDTH : n_in + 11 + WIDTH]
    depth_ref, grad_ref, coef_ref, mom_ref, ip_ref, term_ref, blocks_ref, sems = refs[n_in + 11 + WIDTH :]
    kappa = 2.0 / PIX

    def fetch(step):
        cols = pl.ds(pl.multiple_of(step * NB, 128), NB)
        return pltpu.make_async_copy(crows_ref.at[:, cols], blocks_ref.at[step], sems.at[step])

    for step in range(STEPS):
        fetch(step).start()

    def hot_of():
        return (iota((16, TERMS), 0) == sides_row_ref[...]).astype(F32)

    def term_rows():
        return [term_ref[i : i + 1, :] for i in range(16)]

    ip_ref[...] = jnp.zeros_like(ip_ref)

    def take(value, k):
        value = value.astype(F32)
        depth_ref[pl.ds(pl.multiple_of(k * RS, 8), CHUNKS), :] = value[0:CHUNKS]
        ip_ref[pl.ds(k, 1), :] = value[CHUNKS : CHUNKS + 1]

    if pick:
        own_ref, far_ref, other_ref, passed_ref = bufs[:4]
        near_refs = bufs[4:]
        side = 1 - 2 * lax.rem(lax.axis_index("dev"), 2)
        take(own_ref[fetch_ref[0, REACH]], REACH)
        take(far_ref[fetch_ref[0, 2 * REACH]], 2 * REACH)
        take(other_ref[fetch_ref[0, REACH + side]], REACH + side)
        for i, chip in enumerate(CHIPS):
            if REACH + 2 * chip < 2 * REACH:
                take(near_refs[i][fetch_ref[0, REACH + 2 * chip]], REACH + 2 * chip)
            k = REACH + 2 * chip + side

            @pl.when((k >= 0) & (k < 2 * REACH))
            def _():
                take(passed_ref[i], k)

    else:
        for k in range(WIDTH):
            take(bufs[k][...], k)
    mom_ref[...] = jnp.zeros_like(mom_ref)
    hot = hot_of()
    images = lax.dot_general(ip_ref[...], hot, (((0,), (0,)), ((), ())), precision=HIGH, preferred_element_type=F32)
    spread = (iota((24, TERMS), 0) == iota((24, TERMS), 1) // 2).astype(F32)
    pairs = nn(pp_ref[...], spread, HIGH)
    term_ref[0:8, :] = images[0:8, :]
    term_ref[8:15, :] = pairs
    t = term_rows()
    rot, _ = rotation(t[0:3])
    turn, _ = rotation(t[8:11])
    sigma = jnp.exp(t[14])
    live = (iota((1, TERMS), 1) // 2 < live_ref[0]).astype(F32) * kappa
    tau = [t[3 + a] - sigma * t[11 + a] for a in range(3)]
    zero = jnp.zeros((16, TERMS), F32)
    blocks = []
    for j in range(3):
        a_j = (rot[0][j] * tau[0] + rot[1][j] * tau[1] + rot[2][j] * tau[2]) * live
        b_j = [
            -(rot[0][j] * turn[0][d] + rot[1][j] * turn[1][d] + rot[2][j] * turn[2][d]) * sigma * live
            for d in range(3)
        ]
        blocks.append([hot * a_j] + [hot * b for b in b_j])
    blocks.append([hot * live, zero, zero, zero])
    for j in range(4):
        for n in range(4):
            high, low = split(blocks[j][n])
            for where in ([n] if n == 0 else [n, n + 3]):
                coef_ref[16 * j : 16 * j + 16, where * TERMS : (where + 1) * TERMS] = high
                coef_ref[64 + 16 * j : 80 + 16 * j, where * TERMS : (where + 1) * TERMS] = low

    def block(step, carry):
        fetch(step).wait()
        pos = (iota((8, NB), 1) + step * NB).astype(F32)
        row = jnp.floor((pos + 0.5) * (1.0 / IMG_SIDE))
        x = pos - row * IMG_SIDE - (IMG_SIDE - 1) / 2.0
        y = row - (IMG_SIDE - 1) / 2.0
        near = jnp.concatenate([depth_ref[pl.ds(step * SUB + c, 8, stride=RS), :] for c in range(SUB)], axis=1)
        far = jnp.concatenate([depth_ref[pl.ds(8 * RS + step * SUB + c, 1), :] for c in range(SUB)], axis=1)
        near = jnp.exp(near)
        far = jnp.exp(far)
        near2 = near * near
        fields = [near, near * x, near * y, near2, near2 * x, near2 * y]
        fields += [fields[4] * x, fields[4] * y, fields[5] * y]
        sub = iota((8, NB), 0)
        farb = jnp.broadcast_to(far, (8, NB))
        base = jnp.where(sub < 3, farb, farb * farb)
        first_w = jnp.where((sub == 1) | (sub == 4), x, jnp.where((sub == 2) | (sub == 5), y, 1.0))
        first_w = jnp.where(sub >= 6, x, first_w)
        second_w = jnp.where(sub == 6, x, jnp.where(sub == 7, y, 1.0))
        fields.append(base * first_w * second_w)
        fields.append(jnp.where(sub == 0, farb * farb * y * y, jnp.where(sub == 1, 1.0, 0.0)))
        tiles = []
        for value in fields:
            high, low = split(value)
            tiles.append(jnp.concatenate([high, low], axis=0).astype(BF16))
        stack = jnp.concatenate(tiles, axis=0)
        conf = blocks_ref[step, 0:TERMS, :]
        conf_wide = conf.astype(F32)
        highs = []
        lows = []
        for d in range(3):
            high, low = split(conf_wide * blocks_ref[step, (1 + d) * TERMS : (2 + d) * TERMS, :].astype(F32))
            highs.append(high.astype(BF16))
            lows.append(low.astype(BF16))
        crows = jnp.concatenate([conf] + highs + lows, axis=0)
        mom_ref[...] += nt(crows, stack)

        out = nn(coef_ref[...].astype(BF16), crows)
        out = out[0:64] + out[64:128]
        inv_f = 1.0 / (focal_base * jnp.exp(ip_ref[:, 6:7]))
        near_f = inv_f[0:8]
        far_f = inv_f[8:9]
        rr = x * x + y * y
        near_g = near * (near * (rr * (near_f * near_f) + 1.0) * out[48:56] + (x * out[0:8] + y * out[16:24]) * near_f + out[32:40])
        far_g = far * (
            far * (rr[0:1] * (far_f * far_f) + 1.0) * out[56:57] + (x[0:1] * out[8:9] + y[0:1] * out[24:25]) * far_f + out[40:41]
        )
        for c in range(SUB):
            grad_ref[pl.ds(step * SUB + c, 8, stride=RS), :] = near_g[:, 128 * c : 128 * c + 128]
            grad_ref[pl.ds(8 * RS + step * SUB + c, 1), :] = far_g[:, 128 * c : 128 * c + 128]
        return carry

    lax.fori_loop(0, STEPS, block, 0)

    col = iota((TERMS, FCOLS), 1)
    image_of = jnp.where(col < 144, col % 8, 8)
    mask = ((image_of == sides_col_ref[...]) | (col == 161)).astype(F32)
    fcol = iota((16, FCOLS), 1)
    inside = jnp.where(
        fcol < 144,
        fcol // 16,
        jnp.where(fcol < 160, fcol % 8, jnp.where(fcol % 8 == 0, 8, jnp.where(fcol == 161, 9, 20))),
    )
    pickf = (inside == iota((16, FCOLS), 0)).astype(F32)
    groups = [nt(pickf, mom_ref[0:TERMS, :] * mask, HIGH)]
    for d in range(3):
        both = mom_ref[(1 + d) * TERMS : (2 + d) * TERMS, :] + mom_ref[(4 + d) * TERMS : (5 + d) * TERMS, :]
        groups.append(nt(pickf, both * mask, HIGH))
    eye = (iota((8, 128), 0) == iota((8, 128), 1)).astype(F32)
    pp = nt(eye, sums_ref[...], HIGH)

    def at(group, field):
        return groups[group][field : field + 1, :]

    t = term_rows()
    rot, rot_s = rotation(t[0:3])
    turn, turn_s = rotation(t[8:11])
    sigma = jnp.exp(t[14])
    inv = 1.0 / (focal_base * jnp.exp(t[6]))
    inv2 = inv * inv
    live = (iota((1, TERMS), 1) // 2 < live_ref[0]).astype(F32) * kappa
    tau = [t[3 + a] - sigma * t[11 + a] for a in range(3)]
    c1 = at(0, 9)
    m1 = [at(0, 1) * inv, at(0, 2) * inv, at(0, 0)]
    qxx, qxy, qyy = at(0, 6) * inv2, at(0, 7) * inv2, at(0, 8) * inv2
    qx, qy, q1 = at(0, 4) * inv, at(0, 5) * inv, at(0, 3)
    q = [[qxx, qxy, qx], [qxy, qyy, qy], [qx, qy, q1]]
    p1 = [at(1 + d, 9) for d in range(3)]
    nd = [[at(1 + d, 1) * inv, at(1 + d, 2) * inv, at(1 + d, 0)] for d in range(3)]
    order = {}
    j = 0
    for a in range(3):
        for b in range(a, 3):
            order[(a, b)] = order[(b, a)] = j
            j += 1
    ppm = [[pp[order[(a, b)] : order[(a, b)] + 1, :] for b in range(3)] for a in range(3)]
    three = range(3)
    sturn = [[sigma * turn[a][d] for d in three] for a in three]
    s0 = [
        (sum(rot[a][j] * m1[j] for j in three) + tau[a] * c1 - sum(sturn[a][d] * p1[d] for d in three)) * live
        for a in three
    ]
    s1 = [
        [
            (sum(rot[a][l] * q[l][j] for l in three) + tau[a] * m1[j] - sum(sturn[a][d] * nd[d][j] for d in three)) * live
            for j in three
        ]
        for a in three
    ]
    s2 = [
        [
            (sum(rot[a][j] * nd[d][j] for j in three) + tau[a] * p1[d] - sum(sturn[a][b] * ppm[b][d] for b in three)) * live
            for d in three
        ]
        for a in three
    ]
    image_g = rotation_grad(t[0:3], rot, rot_s, s1) + s0
    image_g.append(-sum(rot[a][j] * s1[a][j] for a in three for j in range(2)))
    turn_g = [[-sigma * s2[a][d] for d in three] for a in three]
    pair_g = rotation_grad(t[8:11], turn, turn_s, turn_g) + [-sigma * s0[a] for a in three]
    pair_g.append(
        -sigma * (sum(turn[a][d] * s2[a][d] for a in three for d in three) + sum(t[11 + a] * s0[a] for a in three))
    )
    for i in range(7):
        term_ref[i : i + 1, :] = image_g[i]
        term_ref[8 + i : 9 + i, :] = pair_g[i]
    hot = hot_of()
    image_sum = nt(hot, term_ref[0:8, :], HIGH)
    join = (iota((24, TERMS), 0) == iota((24, TERMS), 1) // 2).astype(F32)
    pair_sum = nt(term_ref[8:16, :], join, HIGH)[0:7]
    new_p, new_m, new_v = adam(pp_ref[...], pair_sum, pm_ref[...], pv_ref[...], count_step)
    npp_ref[...] = new_p
    npm_ref[...] = new_m
    npv_ref[...] = new_v
    ip_ref[...] = jnp.zeros_like(ip_ref)
    ip_ref[:, 0:8] = image_sum
    pad = jnp.zeros((PROW - CHUNKS, 128), F32)
    for k in range(WIDTH):
        row = jnp.where(iota((1, 128), 1) == ASK, fetch_ref[0, k].astype(F32), ip_ref[k : k + 1, :])
        tail = jnp.where(iota((PROW - CHUNKS, 128), 0) == 0, row, pad)
        outs[k][...] = jnp.concatenate([grad_ref[k * RS : k * RS + CHUNKS, :], tail], axis=0).astype(BF16)


def grads(count, pick, fetch, bufs, crows, sums, sides_col, sides_row, live, pp, pm, pv):
    payload = pair = vm = pl.BlockSpec(memory_space=pltpu.VMEM)
    return pl.pallas_call(
        lambda *refs: grads_kernel(count, pick, *refs),
        in_specs=[pl.BlockSpec(memory_space=pltpu.SMEM)]
        + [payload] * len(bufs)
        + [
            pl.BlockSpec(memory_space=pltpu.HBM),
            vm,
            vm,
            vm,
            pl.BlockSpec(memory_space=pltpu.SMEM),
            pair,
            pair,
            pair,
        ],
        out_specs=[payload] * WIDTH + [pair] * 3,
        out_shape=[jax.ShapeDtypeStruct((PROW, 128), BF16)] * WIDTH + [jax.ShapeDtypeStruct((7, 24), F32)] * 3,
        scratch_shapes=[
            pltpu.VMEM((WIDTH * RS, 128), F32),
            pltpu.VMEM((WIDTH * RS, 128), F32),
            pltpu.VMEM((128, CROWS), F32),
            pltpu.VMEM((CROWS, FCOLS), F32),
            pltpu.VMEM((16, 128), F32),
            pltpu.VMEM((16, TERMS), F32),
            pltpu.VMEM((STEPS, 4 * TERMS, NB), BF16),
            pltpu.SemaphoreType.DMA((STEPS,)),
        ],
        compiler_params=pltpu.CompilerParams(vmem_limit_bytes=20 << 20),
        cost_estimate=pl.CostEstimate(flops=2_500_000_000, bytes_accessed=9_000_000, transcendentals=200_000),
        name="grads",
    )(fetch, *bufs, crows, sums, sides_col, sides_row, live, pp, pm, pv)


def on_device(
    log_depth, depth_m, depth_v, image_params, image_m, image_v,
    pair_points, pair_conf, pair_params, pair_m, pair_v, fetch, pair_sides, pair_count,
):
    devices_n = lax.axis_size("dev")
    offsets = [k - REACH for k in range(2 * REACH)] + [devices_n // 2]

    def shift(value, off):
        if off == 0:
            return value
        return lax.ppermute(value, "dev", [(i, (i + off) % devices_n) for i in range(devices_n)])

    points = pltpu.with_memory_space_constraint(pair_points.transpose(0, 2, 1, 3), pltpu.HBM)
    crows, sums = prepare(points, pltpu.with_memory_space_constraint(pair_conf, pltpu.HBM))
    sides_row = pair_sides.reshape(1, TERMS)
    sides_col = pair_sides.reshape(TERMS, 1)

    def wide(value):
        return jnp.pad(value.T, ((0, 0), (0, 121)))

    ip, im, iv = wide(image_params), wide(image_m), wide(image_v)
    images = pack(log_depth, ip)
    swap = [(i, i ^ 1) for i in range(devices_n)]
    other_asks = lax.ppermute(fetch, "dev", swap)
    other = lax.ppermute(images, "dev", swap)
    near = [shift(images, -2 * chip) for chip in CHIPS]
    far = shift(images, devices_n // 2)
    passed = lax.ppermute(forward(other_asks, sums, near), "dev", swap)
    direct = [value for value, chip in zip(near, CHIPS) if 2 * chip < REACH]
    bufs = [images, far, other, passed] + direct
    for step_id in range(ITERS):
        count = adam_start + step_id + 1
        last = step_id == ITERS - 1
        if step_id > 0:
            bufs = [shift(out[k], -offsets[k]) for k in range(WIDTH)]
        res = grads(count, step_id == 0, fetch, bufs, pltpu.with_memory_space_constraint(crows, pltpu.HBM), sums, sides_col, sides_row, pair_count, pair_params, pair_m, pair_v)
        back = [shift(res[k], offsets[k]) for k in range(WIDTH)]
        pair_params, pair_m, pair_v = res[WIDTH:]
        res = update(count, last, back, log_depth, depth_m, depth_v, ip, im, iv)
        if last:
            log_depth, ip = res
        else:
            log_depth, ip, depth_m, depth_v, im, iv = res[:6]
            out = res[6:]
    return (log_depth, ip[:, 0:7].T, pair_params)


def solution(mesh):
    return jax.shard_map(
        on_device,
        mesh=mesh,
        in_specs=(
            P("dev", None),
            P("dev", None),
            P("dev", None),
            P(None, "dev"),
            P(None, "dev"),
            P(None, "dev"),
            P("dev", None, None, None),
            P("dev", None, None),
            P(None, "dev"),
            P(None, "dev"),
            P(None, "dev"),
            P("dev", None),
            P("dev", None),
            P("dev"),
        ),
        out_specs=(P("dev", None), P(None, "dev"), P(None, "dev")),
        check_vma=False,
    )
```

```python
import jax
import jax.numpy as jnp
from jax import lax
from jax.experimental import pallas as pl
from jax.experimental.pallas import tpu as pltpu
from jax.sharding import PartitionSpec as P

IMG_SIDE = 112
PIX = 12544
REACH = 4
ITERS = 2
WIDTH = 2 * REACH + 1
CHUNKS = PIX // 128
PROW = 104
ASK = 8
RS = 104
NB = 1792
STEPS = PIX // NB
SUB = NB // 128
SLOTS = 24
TERMS = 2 * SLOTS
CROWS = 7 * TERMS
FCOLS = 176

focal_base = 100.0
learn_rate = 0.05
beta_one = 0.9
beta_two = 0.999
adam_epsilon = 1e-08
adam_start = 20


CHIPS = (-2, -1, 1, 2)

F32 = jnp.float32
BF16 = jnp.bfloat16
HIGH = lax.Precision.HIGHEST


def adam(param, grad, moment, second, count):
    moment = beta_one * moment + (1.0 - beta_one) * grad
    second = beta_two * second + (1.0 - beta_two) * grad * grad
    fix_one = 1.0 - beta_one**count
    fix_two = 1.0 - beta_two**count
    step = (learn_rate / fix_one) * moment / (jnp.sqrt(second * (1.0 / fix_two)) + adam_epsilon)
    return param - step, moment, second


def rotation(vec):
    x, y, z = vec
    s = 1.0 / (1.0 + x * x + y * y + z * z)
    return [
        [(1.0 + x * x - y * y - z * z) * s, 2.0 * (x * y - z) * s, 2.0 * (x * z + y) * s],
        [2.0 * (x * y + z) * s, (1.0 - x * x + y * y - z * z) * s, 2.0 * (y * z - x) * s],
        [2.0 * (x * z - y) * s, 2.0 * (y * z + x) * s, (1.0 - x * x - y * y + z * z) * s],
    ], s


def rotation_grad(vec, rot, s, g):
    x, y, z = vec
    inner = sum(g[i][j] * rot[i][j] for i in range(3) for j in range(3))
    s2 = 2.0 * s
    gx = x * (g[0][0] - g[1][1] - g[2][2]) + y * (g[0][1] + g[1][0]) + z * (g[0][2] + g[2][0]) + (g[2][1] - g[1][2])
    gy = y * (g[1][1] - g[0][0] - g[2][2]) + x * (g[0][1] + g[1][0]) + z * (g[1][2] + g[2][1]) + (g[0][2] - g[2][0])
    gz = z * (g[2][2] - g[0][0] - g[1][1]) + x * (g[0][2] + g[2][0]) + y * (g[1][2] + g[2][1]) + (g[1][0] - g[0][1])
    return [s2 * (gx - x * inner), s2 * (gy - y * inner), s2 * (gz - z * inner)]


def split(value):
    high = value.astype(BF16).astype(F32)
    return high, value - high


def nt(lhs, rhs, precision=None):
    return lax.dot_general(lhs, rhs, (((1,), (1,)), ((), ())), precision=precision, preferred_element_type=F32)


def nn(lhs, rhs, precision=None):
    return lax.dot_general(lhs, rhs, (((1,), (0,)), ((), ())), precision=precision, preferred_element_type=F32)


def tn(lhs, rhs):
    return lax.dot_general(lhs, rhs, (((0,), (0,)), ((), ())), precision=HIGH, preferred_element_type=F32)


def by_image(params):
    return tn(params, (iota((7, 128), 0) == iota((7, 128), 1)).astype(F32))


def by_param(rows):
    return tn(rows, (iota((8, 8), 0) == iota((8, 8), 1)).astype(F32))[0:7]


def iota(shape, dim):
    return lax.broadcasted_iota(jnp.int32, shape, dim)


def prepare_kernel(points_ref, conf_ref, out_ref, sums_ref, acc_ref):
    step = pl.program_id(0)

    @pl.when(step == 0)
    def _():
        acc_ref[...] = jnp.zeros_like(acc_ref)

    conf = conf_ref[...].astype(F32).reshape(TERMS, NB).astype(BF16)
    out_ref[0:TERMS, :] = conf
    conf = conf.astype(F32)
    pts = []
    for d in range(3):
        rows = points_ref[:, d].astype(F32).reshape(TERMS, NB).astype(BF16)
        out_ref[(1 + d) * TERMS : (2 + d) * TERMS, :] = rows
        pts.append(rows.astype(F32))
    weighted = [conf * pts[d] for d in range(3)]
    j = 0
    for a in range(3):
        for b in range(a, 3):
            prod = weighted[a] * pts[b]
            total = prod[:, 0:128]
            for c in range(1, SUB):
                total = total + prod[:, c * 128 : (c + 1) * 128]
            acc_ref[j] += total
            j += 1

    @pl.when(step == STEPS - 1)
    def _():
        lane = iota((TERMS, 128), 1)
        res = jnp.zeros((TERMS, 128), F32)
        for i in range(6):
            res = jnp.where(lane == i, jnp.sum(acc_ref[i], axis=1, keepdims=True), res)
        sums_ref[...] = res


def prepare(points, conf):
    return pl.pallas_call(
        prepare_kernel,
        grid=(STEPS,),
        in_specs=[
            pl.BlockSpec((SLOTS, 3, 2, NB), lambda i: (0, 0, 0, i)),
            pl.BlockSpec((SLOTS, 2, NB), lambda i: (0, 0, i)),
        ],
        out_specs=[
            pl.BlockSpec((4 * TERMS, NB), lambda i: (0, i)),
            pl.BlockSpec((TERMS, 128), lambda i: (0, 0)),
        ],
        out_shape=[
            pltpu.HBM((4 * TERMS, PIX), BF16),
            jax.ShapeDtypeStruct((TERMS, 128), F32),
        ],
        scratch_shapes=[pltpu.VMEM((6, TERMS, 128), F32)],
        compiler_params=pltpu.CompilerParams(vmem_limit_bytes=16 << 20),
        cost_estimate=pl.CostEstimate(flops=20_000_000, bytes_accessed=14_000_000, transcendentals=0),
        name="prepare",
    )(points, conf)


def payload_of(rows_ref, param_rows, image):
    pixels = rows_ref[pl.ds(image, CHUNKS, stride=8), :]
    row = param_rows[pl.ds(image, 1), :]
    tail = jnp.where(iota((PROW - CHUNKS, 128), 0) == 0, row, 0.0)
    return jnp.concatenate([pixels, tail], axis=0).astype(BF16)


def pack_kernel(depth_hbm, param_hbm, out_ref, rows_ref, wide_ref, depth_ref, param_ref, sems):
    depth_copy = pltpu.make_async_copy(depth_hbm, depth_ref, sems.at[0])
    param_copy = pltpu.make_async_copy(param_hbm, param_ref, sems.at[1])
    depth_copy.start()
    param_copy.start()
    param_copy.wait()
    wide_ref[0:8, :] = by_image(param_ref[...])
    depth_copy.wait()
    for c in range(CHUNKS):
        rows_ref[8 * c : 8 * c + 8, :] = depth_ref[:, 128 * c : 128 * c + 128]
    for image in range(8):
        out_ref[image] = payload_of(rows_ref, wide_ref, image)


def pack(depth, params):
    vm = pl.BlockSpec(memory_space=pltpu.VMEM)
    return pl.pallas_call(
        pack_kernel,
        in_specs=[pl.BlockSpec(memory_space=pltpu.HBM)] * 2,
        out_specs=vm,
        out_shape=jax.ShapeDtypeStruct((8, PROW, 128), BF16),
        scratch_shapes=[
            pltpu.VMEM((8 * RS, 128), F32),
            pltpu.VMEM((16, 128), F32),
            pltpu.VMEM((8, PIX), F32),
            pltpu.VMEM((7, 8), F32),
            pltpu.SemaphoreType.DMA((2,)),
        ],
        compiler_params=pltpu.CompilerParams(vmem_limit_bytes=8 << 20),
        cost_estimate=pl.CostEstimate(flops=1_000_000, bytes_accessed=700_000, transcendentals=0),
        name="pack",
    )(pltpu.with_memory_space_constraint(depth, pltpu.HBM), pltpu.with_memory_space_constraint(params, pltpu.HBM))


def forward_kernel(ask_ref, after_ref, *refs):
    del after_ref
    bufs = refs[: len(CHIPS)]
    out_ref = refs[len(CHIPS)]
    side = 1 - 2 * lax.rem(lax.axis_index("dev"), 2)
    for i, chip in enumerate(CHIPS):
        k = jnp.clip(REACH + 2 * chip - side, 0, 2 * REACH - 1)
        out_ref[i] = bufs[i][ask_ref[0, k]]


def forward(ask, after, bufs):
    vm = pl.BlockSpec(memory_space=pltpu.VMEM)
    return pl.pallas_call(
        forward_kernel,
        in_specs=[pl.BlockSpec(memory_space=pltpu.SMEM)] + [vm] * (len(CHIPS) + 1),
        out_specs=vm,
        out_shape=jax.ShapeDtypeStruct((len(CHIPS), PROW, 128), BF16),
        compiler_params=pltpu.CompilerParams(vmem_limit_bytes=4 << 20),
        cost_estimate=pl.CostEstimate(flops=1_000, bytes_accessed=230_000, transcendentals=0),
        name="forward",
    )(ask, after, *bufs)


def update_kernel(count, last, *refs):
    back = refs[:WIDTH]
    depth_ref, m_ref, v_ref, ip_ref, im_ref, iv_ref = refs[WIDTH : WIDTH + 6]
    rest = refs[WIDTH + 6 :]
    n_out = 2 if last else 6 + WIDTH
    outs = rest[:n_out]
    acc_ref, pacc_ref = rest[n_out : n_out + 2]
    acc_ref[...] = jnp.zeros_like(acc_ref)
    pacc_ref[...] = jnp.zeros_like(pacc_ref)
    lane = iota((1, 128), 1)
    served = []
    for k in range(WIDTH):
        row = back[k][CHUNKS:PROW, :].astype(F32)[0:1]
        served.append(jnp.sum(jnp.where(lane == ASK, row, 0.0)).astype(jnp.int32))
    for k in range(WIDTH):
        image = served[k]
        value = back[k][...].astype(F32)
        where = pl.ds(image, CHUNKS, stride=8)
        acc_ref[where, :] = acc_ref[where, :] + value[0:CHUNKS]
        row = jnp.where(lane < ASK, value[CHUNKS : CHUNKS + 1], 0.0)
        pacc_ref[pl.ds(image, 1), :] = pacc_ref[pl.ds(image, 1), :] + row
    for c in range(CHUNKS):
        cols = slice(128 * c, 128 * c + 128)
        rows = slice(8 * c, 8 * c + 8)
        depth, m, v = adam(depth_ref[:, cols], acc_ref[rows, :], m_ref[:, cols], v_ref[:, cols], count)
        outs[0][:, cols] = depth
        if not last:
            outs[2][:, cols] = m
            outs[3][:, cols] = v
            acc_ref[rows, :] = depth
    states = [ref[...] if last else by_image(ref[...]) for ref in (ip_ref, im_ref, iv_ref)]
    param, pm, pv = adam(states[0], pacc_ref[0:8, :], states[1], states[2], count)
    outs[1][...] = by_param(param) if last else param
    if not last:
        outs[4][...] = pm
        outs[5][...] = pv
        pacc_ref[0:8, :] = param
        for k in range(WIDTH):
            outs[6 + k][...] = payload_of(acc_ref, pacc_ref, served[k])


def update(count, last, back, depth, m, v, ip, im, iv):
    big = jax.ShapeDtypeStruct((8, PIX), F32)
    small = jax.ShapeDtypeStruct((8, 128), F32)
    shapes = [big, jax.ShapeDtypeStruct((7, 8), F32)] if last else [big, small, big, big, small, small] + [jax.ShapeDtypeStruct((PROW, 128), BF16)] * WIDTH
    vm = pl.BlockSpec(memory_space=pltpu.VMEM)
    return pl.pallas_call(
        lambda *refs: update_kernel(count, last, *refs),
        in_specs=[vm] * (WIDTH + 6),
        out_specs=[vm] * len(shapes),
        out_shape=shapes,
        scratch_shapes=[pltpu.VMEM((8 * RS, 128), F32), pltpu.VMEM((16, 128), F32)],
        compiler_params=pltpu.CompilerParams(vmem_limit_bytes=8 << 20),
        cost_estimate=pl.CostEstimate(flops=3_000_000, bytes_accessed=2_500_000, transcendentals=0),
        name="update",
    )(*back, depth, m, v, ip, im, iv)


def grads_kernel(count_step, pick, fetch_ref, *refs):
    n_in = 4 + len([c for c in CHIPS if 2 * c < REACH]) if pick else WIDTH
    bufs = refs[:n_in]
    crows_ref, sums_ref, sides_col_ref, sides_row_ref, live_ref, pp_ref, pm_ref, pv_ref = refs[n_in : n_in + 8]
    outs = refs[n_in + 8 : n_in + 8 + WIDTH]
    npp_ref, npm_ref, npv_ref = refs[n_in + 8 + WIDTH : n_in + 11 + WIDTH]
    depth_ref, grad_ref, coef_ref, mom_ref, ip_ref, term_ref, blocks_ref, sems = refs[n_in + 11 + WIDTH :]
    kappa = 2.0 / PIX

    def fetch(step):
        cols = pl.ds(pl.multiple_of(step * NB, 128), NB)
        return pltpu.make_async_copy(crows_ref.at[:, cols], blocks_ref.at[step], sems.at[step])

    for step in range(STEPS):
        fetch(step).start()

    def hot_of():
        return (iota((16, TERMS), 0) == sides_row_ref[...]).astype(F32)

    def term_rows():
        return [term_ref[i : i + 1, :] for i in range(16)]

    ip_ref[...] = jnp.zeros_like(ip_ref)

    def take(value, k):
        value = value.astype(F32)
        depth_ref[pl.ds(pl.multiple_of(k * RS, 8), CHUNKS), :] = value[0:CHUNKS]
        ip_ref[pl.ds(k, 1), :] = value[CHUNKS : CHUNKS + 1]

    if pick:
        own_ref, far_ref, other_ref, passed_ref = bufs[:4]
        near_refs = bufs[4:]
        side = 1 - 2 * lax.rem(lax.axis_index("dev"), 2)
        take(own_ref[fetch_ref[0, REACH]], REACH)
        take(far_ref[fetch_ref[0, 2 * REACH]], 2 * REACH)
        take(other_ref[fetch_ref[0, REACH + side]], REACH + side)
        for i, chip in enumerate(CHIPS):
            if REACH + 2 * chip < 2 * REACH:
                take(near_refs[i][fetch_ref[0, REACH + 2 * chip]], REACH + 2 * chip)
            k = REACH + 2 * chip + side

            @pl.when((k >= 0) & (k < 2 * REACH))
            def _():
                take(passed_ref[i], k)

    else:
        for k in range(WIDTH):
            take(bufs[k][...], k)
    mom_ref[...] = jnp.zeros_like(mom_ref)
    hot = hot_of()
    images = lax.dot_general(ip_ref[...].astype(BF16), hot.astype(BF16), (((0,), (0,)), ((), ())), preferred_element_type=F32)
    spread = (iota((24, TERMS), 0) == iota((24, TERMS), 1) // 2).astype(F32)
    pairs = nn(pp_ref[...], spread, HIGH)
    term_ref[0:8, :] = images[0:8, :]
    term_ref[8:15, :] = pairs
    t = term_rows()
    rot, _ = rotation(t[0:3])
    turn, _ = rotation(t[8:11])
    sigma = jnp.exp(t[14])
    live = (iota((1, TERMS), 1) // 2 < live_ref[0]).astype(F32) * kappa
    tau = [t[3 + a] - sigma * t[11 + a] for a in range(3)]
    zero = jnp.zeros((1, TERMS), F32)
    blocks = []
    for j in range(3):
        a_j = (rot[0][j] * tau[0] + rot[1][j] * tau[1] + rot[2][j] * tau[2]) * live
        b_j = [
            -(rot[0][j] * turn[0][d] + rot[1][j] * turn[1][d] + rot[2][j] * turn[2][d]) * sigma * live
            for d in range(3)
        ]
        blocks.append([a_j] + b_j)
    blocks.append([live, zero, zero, zero])
    coef_ref[...] = jnp.zeros_like(coef_ref)
    for j in range(4):
        for n in range(4):
            high, low = split(hot * blocks[j][n])
            for where in [n] if n == 0 else [n, n + 3]:
                cols = slice(where * TERMS, (where + 1) * TERMS)
                coef_ref[8 * j : 8 * j + 8, cols] = high[0:8]
                coef_ref[32 + j : 33 + j, cols] = high[8:9]
                coef_ref[40 + 8 * j : 48 + 8 * j, cols] = low[0:8]
                coef_ref[72 + j : 73 + j, cols] = low[8:9]

    def block(step, carry):
        fetch(step).wait()
        pos = (iota((8, NB), 1) + step * NB).astype(F32)
        row = jnp.floor((pos + 0.5) * (1.0 / IMG_SIDE))
        x = pos - row * IMG_SIDE - (IMG_SIDE - 1) / 2.0
        y = row - (IMG_SIDE - 1) / 2.0
        near = jnp.concatenate([depth_ref[pl.ds(step * SUB + c, 8, stride=RS), :] for c in range(SUB)], axis=1)
        far = jnp.concatenate([depth_ref[pl.ds(8 * RS + step * SUB + c, 1), :] for c in range(SUB)], axis=1)
        near = jnp.exp(near)
        far = jnp.exp(far)
        near2 = near * near
        fields = [near, near * x, near * y, near2, near2 * x, near2 * y]
        fields += [fields[4] * x, fields[4] * y, fields[5] * y]
        sub = iota((8, NB), 0)
        farb = jnp.broadcast_to(far, (8, NB))
        base = jnp.where(sub < 3, farb, farb * farb)
        first_w = jnp.where((sub == 1) | (sub == 4), x, jnp.where((sub == 2) | (sub == 5), y, 1.0))
        first_w = jnp.where(sub >= 6, x, first_w)
        second_w = jnp.where(sub == 6, x, jnp.where(sub == 7, y, 1.0))
        fields.append(base * first_w * second_w)
        fields.append(jnp.where(sub == 0, farb * farb * y * y, jnp.where(sub == 1, 1.0, 0.0)))
        tiles = []
        for value in fields:
            high, low = split(value)
            tiles.append(jnp.concatenate([high, low], axis=0).astype(BF16))
        stack = jnp.concatenate(tiles, axis=0)
        conf = blocks_ref[step, 0:TERMS, :]
        conf_wide = conf.astype(F32)
        highs = []
        lows = []
        for d in range(3):
            high, low = split(conf_wide * blocks_ref[step, (1 + d) * TERMS : (2 + d) * TERMS, :].astype(F32))
            highs.append(high.astype(BF16))
            lows.append(low.astype(BF16))
        crows = jnp.concatenate([conf] + highs + lows, axis=0)
        mom_ref[...] += nt(crows, stack)

        out = nn(coef_ref[...].astype(BF16), crows)
        out = out[0:40] + out[40:80]
        inv_f = 1.0 / (focal_base * jnp.exp(ip_ref[:, 6:7]))
        near_f = inv_f[0:8]
        far_f = inv_f[8:9]
        rr = x * x + y * y
        near_g = near * (near * (rr * (near_f * near_f) + 1.0) * out[24:32] + (x * out[0:8] + y * out[8:16]) * near_f + out[16:24])
        far_g = far * (
            far * (rr[0:1] * (far_f * far_f) + 1.0) * out[35:36] + (x[0:1] * out[32:33] + y[0:1] * out[33:34]) * far_f + out[34:35]
        )
        for c in range(SUB):
            grad_ref[pl.ds(step * SUB + c, 8, stride=RS), :] = near_g[:, 128 * c : 128 * c + 128]
            grad_ref[pl.ds(8 * RS + step * SUB + c, 1), :] = far_g[:, 128 * c : 128 * c + 128]
        return carry

    lax.fori_loop(0, STEPS, block, 0)

    col = iota((TERMS, FCOLS), 1)
    image_of = jnp.where(col < 144, col % 8, 8)
    mask = ((image_of == sides_col_ref[...]) | (col == 161)).astype(F32)
    fcol = iota((16, FCOLS), 1)
    inside = jnp.where(
        fcol < 144,
        fcol // 16,
        jnp.where(fcol < 160, fcol % 8, jnp.where(fcol % 8 == 0, 8, jnp.where(fcol == 161, 9, 20))),
    )
    pickf = (inside == iota((16, FCOLS), 0)).astype(F32)
    groups = [nt(pickf, mom_ref[0:TERMS, :] * mask, HIGH)]
    for d in range(3):
        both = mom_ref[(1 + d) * TERMS : (2 + d) * TERMS, :] + mom_ref[(4 + d) * TERMS : (5 + d) * TERMS, :]
        groups.append(nt(pickf, both * mask, HIGH))
    eye = (iota((8, 128), 0) == iota((8, 128), 1)).astype(F32)
    pp = nt(eye, sums_ref[...], HIGH)

    def at(group, field):
        return groups[group][field : field + 1, :]

    t = term_rows()
    rot, rot_s = rotation(t[0:3])
    turn, turn_s = rotation(t[8:11])
    sigma = jnp.exp(t[14])
    inv = 1.0 / (focal_base * jnp.exp(t[6]))
    inv2 = inv * inv
    live = (iota((1, TERMS), 1) // 2 < live_ref[0]).astype(F32) * kappa
    tau = [t[3 + a] - sigma * t[11 + a] for a in range(3)]
    c1 = at(0, 9)
    m1 = [at(0, 1) * inv, at(0, 2) * inv, at(0, 0)]
    qxx, qxy, qyy = at(0, 6) * inv2, at(0, 7) * inv2, at(0, 8) * inv2
    qx, qy, q1 = at(0, 4) * inv, at(0, 5) * inv, at(0, 3)
    q = [[qxx, qxy, qx], [qxy, qyy, qy], [qx, qy, q1]]
    p1 = [at(1 + d, 9) for d in range(3)]
    nd = [[at(1 + d, 1) * inv, at(1 + d, 2) * inv, at(1 + d, 0)] for d in range(3)]
    order = {}
    j = 0
    for a in range(3):
        for b in range(a, 3):
            order[(a, b)] = order[(b, a)] = j
            j += 1
    ppm = [[pp[order[(a, b)] : order[(a, b)] + 1, :] for b in range(3)] for a in range(3)]
    three = range(3)
    sturn = [[sigma * turn[a][d] for d in three] for a in three]
    s0 = [
        (sum(rot[a][j] * m1[j] for j in three) + tau[a] * c1 - sum(sturn[a][d] * p1[d] for d in three)) * live
        for a in three
    ]
    s1 = [
        [
            (sum(rot[a][l] * q[l][j] for l in three) + tau[a] * m1[j] - sum(sturn[a][d] * nd[d][j] for d in three)) * live
            for j in three
        ]
        for a in three
    ]
    s2 = [
        [
            (sum(rot[a][j] * nd[d][j] for j in three) + tau[a] * p1[d] - sum(sturn[a][b] * ppm[b][d] for b in three)) * live
            for d in three
        ]
        for a in three
    ]
    image_g = rotation_grad(t[0:3], rot, rot_s, s1) + s0
    image_g.append(-sum(rot[a][j] * s1[a][j] for a in three for j in range(2)))
    turn_g = [[-sigma * s2[a][d] for d in three] for a in three]
    pair_g = rotation_grad(t[8:11], turn, turn_s, turn_g) + [-sigma * s0[a] for a in three]
    pair_g.append(
        -sigma * (sum(turn[a][d] * s2[a][d] for a in three for d in three) + sum(t[11 + a] * s0[a] for a in three))
    )
    for i in range(7):
        term_ref[i : i + 1, :] = image_g[i]
        term_ref[8 + i : 9 + i, :] = pair_g[i]
    hot = hot_of()
    image_sum = nt(hot, term_ref[0:8, :], HIGH)
    join = (iota((24, TERMS), 0) == iota((24, TERMS), 1) // 2).astype(F32)
    pair_sum = nt(term_ref[8:16, :], join, HIGH)[0:7]
    new_p, new_m, new_v = adam(pp_ref[...], pair_sum, pm_ref[...], pv_ref[...], count_step)
    npp_ref[...] = new_p
    npm_ref[...] = new_m
    npv_ref[...] = new_v
    ip_ref[...] = jnp.zeros_like(ip_ref)
    ip_ref[:, 0:8] = image_sum
    pad = jnp.zeros((PROW - CHUNKS, 128), F32)
    for k in range(WIDTH):
        row = jnp.where(iota((1, 128), 1) == ASK, fetch_ref[0, k].astype(F32), ip_ref[k : k + 1, :])
        tail = jnp.where(iota((PROW - CHUNKS, 128), 0) == 0, row, pad)
        outs[k][...] = jnp.concatenate([grad_ref[k * RS : k * RS + CHUNKS, :], tail], axis=0).astype(BF16)


def grads(count, pick, fetch, bufs, crows, sums, sides_col, sides_row, live, pp, pm, pv):
    payload = pair = vm = pl.BlockSpec(memory_space=pltpu.VMEM)
    return pl.pallas_call(
        lambda *refs: grads_kernel(count, pick, *refs),
        in_specs=[pl.BlockSpec(memory_space=pltpu.SMEM)]
        + [payload] * len(bufs)
        + [
            pl.BlockSpec(memory_space=pltpu.HBM),
            vm,
            vm,
            vm,
            pl.BlockSpec(memory_space=pltpu.SMEM),
            pair,
            pair,
            pair,
        ],
        out_specs=[payload] * WIDTH + [pair] * 3,
        out_shape=[jax.ShapeDtypeStruct((PROW, 128), BF16)] * WIDTH + [jax.ShapeDtypeStruct((7, 24), F32)] * 3,
        scratch_shapes=[
            pltpu.VMEM((WIDTH * RS + 8, 128), F32),
            pltpu.VMEM((WIDTH * RS + 8, 128), F32),
            pltpu.VMEM((80, CROWS), F32),
            pltpu.VMEM((CROWS, FCOLS), F32),
            pltpu.VMEM((16, 128), F32),
            pltpu.VMEM((16, TERMS), F32),
            pltpu.VMEM((STEPS, 4 * TERMS, NB), BF16),
            pltpu.SemaphoreType.DMA((STEPS,)),
        ],
        compiler_params=pltpu.CompilerParams(vmem_limit_bytes=20 << 20),
        cost_estimate=pl.CostEstimate(flops=2_500_000_000, bytes_accessed=9_000_000, transcendentals=200_000),
        name="grads",
    )(fetch, *bufs, crows, sums, sides_col, sides_row, live, pp, pm, pv)


def on_device(
    log_depth, depth_m, depth_v, image_params, image_m, image_v,
    pair_points, pair_conf, pair_params, pair_m, pair_v, fetch, pair_sides, pair_count,
):
    devices_n = lax.axis_size("dev")
    offsets = [k - REACH for k in range(2 * REACH)] + [devices_n // 2]

    def shift(value, off):
        if off == 0:
            return value
        return lax.ppermute(value, "dev", [(i, (i + off) % devices_n) for i in range(devices_n)])

    points = pltpu.with_memory_space_constraint(pair_points.transpose(0, 2, 1, 3), pltpu.HBM)
    crows, sums = prepare(points, pltpu.with_memory_space_constraint(pair_conf, pltpu.HBM))
    sides_row = pair_sides.reshape(1, TERMS)
    sides_col = pair_sides.reshape(TERMS, 1)

    ip, im, iv = image_params, image_m, image_v
    images = pack(log_depth, ip)
    swap = [(i, i ^ 1) for i in range(devices_n)]
    other_asks = lax.ppermute(fetch, "dev", swap)
    other = lax.ppermute(images, "dev", swap)
    near = [shift(images, -2 * chip) for chip in CHIPS]
    far = shift(images, devices_n // 2)
    passed = lax.ppermute(forward(other_asks, sums, near), "dev", swap)
    direct = [value for value, chip in zip(near, CHIPS) if 2 * chip < REACH]
    bufs = [images, far, other, passed] + direct
    for step_id in range(ITERS):
        count = adam_start + step_id + 1
        last = step_id == ITERS - 1
        if step_id > 0:
            bufs = [shift(out[k], -offsets[k]) for k in range(WIDTH)]
        res = grads(count, step_id == 0, fetch, bufs, pltpu.with_memory_space_constraint(crows, pltpu.HBM), sums, sides_col, sides_row, pair_count, pair_params, pair_m, pair_v)
        back = [shift(res[k], offsets[k]) for k in range(WIDTH)]
        pair_params, pair_m, pair_v = res[WIDTH:]
        res = update(count, last, back, log_depth, depth_m, depth_v, ip, im, iv)
        if last:
            log_depth, ip = res
        else:
            log_depth, ip, depth_m, depth_v, im, iv = res[:6]
            out = res[6:]
    return (log_depth, ip, pair_params)


def solution(mesh):
    return jax.shard_map(
        on_device,
        mesh=mesh,
        in_specs=(
            P("dev", None),
            P("dev", None),
            P("dev", None),
            P(None, "dev"),
            P(None, "dev"),
            P(None, "dev"),
            P("dev", None, None, None),
            P("dev", None, None),
            P(None, "dev"),
            P(None, "dev"),
            P(None, "dev"),
            P("dev", None),
            P("dev", None),
            P("dev"),
        ),
        out_specs=(P("dev", None), P(None, "dev"), P(None, "dev")),
        check_vma=False,
    )
```
